32 devices in a mesh: groups: 2 (over x), ctx: 16 (over z, y, core).
Axes of the slice: x: 2, y: 2, z: 4, core: 2. Of those that a mesh axis runs over, the one named last changes fastest.
Arguments:
- queries: bfloat16 [128, 4096], P(('groups', 'ctx')), parts along dimension 0, may hold values from -110 to 110
- keys: bfloat16 [16, 65536, 128], P(None, ('groups', 'ctx')), parts along dimension 1, may hold values from -8 to 8
- values: bfloat16 [16, 65536, 128], P(None, ('groups', 'ctx')), parts along dimension 1, may hold values from -6 to 6
- residual: bfloat16 [128, 5376], P(('groups', 'ctx')), parts along dimension 0, may hold values from -6 to 6
- post_gain: float32 [5376], replicated, may hold values from 0.5 to 1.5
- out_weight: bfloat16 [4096, 5376], P('ctx'), may hold values from -0.09375 to 0.09375
Outputs:
- updated: float32 [128, 5376], P(('groups', 'ctx')), parts along dimension 0
The draws below stay inside these ranges and needn't reach their ends.
There are 2 independent parts, one for each index of `groups`. The reference program is written for one: setup_inputs(seed, part) draws one part's arguments, and reference() takes and returns one part's arrays. A program takes and returns all parts, laid end to end along the dimension named above; an argument that names none is the same for every part. Nothing has to cross between parts.
All inputs are finite; a program needn't handle non-finite values.
Results may differ from the reference program's by a relative error of at most 0.017.
Values may be sent and summed in bfloat16 or wider, within the bound.
No kernel may reach another device: no remote copies, remote signals or barrier semaphores. Data moves between devices by JAX's collectives and lax.ppermute only.
A program may use at most 320 MiB of HBM per device.

```python
import jax
import jax.numpy as jnp
from jax import lax

D = 5376
HEADS = 32
KV_HEADS = 16
HEAD_DIM = 128
UNITS = 64
CONTEXT = 32768
N_CTX = 16


def plant_table(key):
    plant_key = jax.random.fold_in(key, 101)
    signs = jnp.where(jax.random.bernoulli(jax.random.fold_in(plant_key, 1), 0.5, (8, HEAD_DIM)), 1.0, -1.0)
    sizes = jax.random.uniform(jax.random.fold_in(plant_key, 3), (8, HEAD_DIM), jnp.float32, 1.0, 1.5)
    vectors = signs * sizes
    places = jax.random.randint(jax.random.fold_in(plant_key, 2), (8,), 0, CONTEXT // 2) * 2
    target = 120.0 + 40.0 * jnp.arange(8, dtype=jnp.float32)
    key_vectors = 5.0 * vectors
    length_sq = jnp.sum(vectors * key_vectors, axis=1)
    factor = target * jnp.sqrt(168.0) / length_sq
    heads_hit = (2 * jnp.arange(8) + 1) % HEADS
    units_hit = jnp.arange(8) * (UNITS // 8)
    return (vectors, key_vectors, places, target, factor, heads_hit, units_hit)


def draw_keys(key, part):
    base = jnp.clip(jax.random.normal(jax.random.fold_in(key, 11), (KV_HEADS, CONTEXT, HEAD_DIM), jnp.float32), -4.0, 4.0)
    vectors, key_vectors, places, target, factor, heads_hit, units_hit = plant_table(key)
    kv_hit = heads_hit // (HEADS // KV_HEADS)
    base = base.at[kv_hit, places].set(key_vectors)
    base = base.at[kv_hit, places + 1].set(key_vectors * (1.0 - 2.0 / target)[:, None])
    return base.astype(jnp.bfloat16)


def draw_queries(key, part):
    base = jnp.clip(jax.random.normal(jax.random.fold_in(key, 21), (UNITS, HEADS, HEAD_DIM), jnp.float32), -4.0, 4.0)
    vectors, key_vectors, places, target, factor, heads_hit, units_hit = plant_table(key)
    base = base.at[units_hit, heads_hit].set(factor[:, None] * vectors)
    return base.reshape(UNITS, HEADS * HEAD_DIM).astype(jnp.bfloat16)


def steps_of(rng, extent, shards, smallest, largest):
    gain = 1.0
    for dim, parts in shards:
        heights = jax.random.uniform(jax.random.fold_in(jax.random.fold_in(rng, 6), dim), (parts,), jnp.float32, smallest / len(shards), largest / len(shards))
        gain = gain * jnp.repeat(jnp.exp(heights), extent[dim] // parts).reshape((-1,) + (1,) * (len(extent) - 1 - dim))
    return gain


def centred(rng, shape, width, reach, cuts=(), kind=jnp.bfloat16):
    factor_of = steps_of(rng, shape, cuts, -0.22, 0.18) if cuts else 1.0
    entries = jax.random.normal(rng, shape, jnp.float32) * width * factor_of
    return jnp.minimum(jnp.maximum(entries, -reach), reach).astype(kind)


def setup_inputs(seed: int = 0, part: int = 0) -> dict:
    splits = jax.random.split(jax.random.key(seed), 7)
    part_splits = jax.random.split(jax.random.fold_in(splits[6], part), 7)
    return {
        "queries": draw_queries(jax.random.fold_in(jax.random.fold_in(splits[6], part), 71), part),
        "keys": draw_keys(jax.random.fold_in(jax.random.fold_in(splits[6], part), 71), part),
        "values": centred(part_splits[2], (KV_HEADS, CONTEXT, HEAD_DIM), 1.0, 6.0, ((1, 16),)),
        "residual": centred(part_splits[3], (UNITS, D), 1.0, 6.0, ((0, 16),)),
        "post_gain": jnp.clip(1.0 + 0.1 * jax.random.normal(splits[4], (D,), jnp.float32), 0.5, 1.5),
        "out_weight": centred(splits[5], (HEADS * HEAD_DIM, D), (HEADS * HEAD_DIM) ** -0.5, 0.09375, ((0, 16),)),
    }


query_scale = 168.0 ** (-0.5)

def attend_head(operands):
    head_queries, head_keys, head_values = operands
    scores = lax.dot_general(head_queries, head_keys, (((1,), (1,)), ((), ())), preferred_element_type=jnp.float32) * query_scale
    row_max = lax.optimization_barrier(jnp.max(scores, axis=1, keepdims=True))
    exponent = jnp.exp(scores - row_max)
    row_total = lax.optimization_barrier(jnp.sum(exponent, axis=1, keepdims=True))
    weights = exponent.astype(jnp.bfloat16)
    weighted = jnp.dot(weights, head_values, preferred_element_type=jnp.float32)
    return (weighted / row_total).astype(jnp.bfloat16)

def reference(queries, keys, values, residual, post_gain, out_weight):
    unit_count = queries.shape[0]
    group_size = HEADS // KV_HEADS
    grouped = queries.reshape(unit_count, KV_HEADS, group_size, HEAD_DIM).transpose(1, 0, 2, 3).reshape(KV_HEADS, unit_count * group_size, HEAD_DIM)
    attended = lax.map(attend_head, (grouped, keys, values))
    attended = attended.reshape(KV_HEADS, unit_count, group_size, HEAD_DIM).transpose(1, 0, 2, 3).reshape(unit_count, HEADS * HEAD_DIM)
    shard_width = HEADS * HEAD_DIM // N_CTX
    pieces = attended.reshape(unit_count, N_CTX, shard_width).transpose(1, 0, 2)
    weight_pieces = out_weight.reshape(N_CTX, shard_width, D)

    def accumulate(carry, operands):
        piece, weight_piece = operands
        term = jnp.dot(piece, weight_piece, preferred_element_type=jnp.float32).astype(jnp.bfloat16)
        term = lax.optimization_barrier(term)
        return (carry + term.astype(jnp.float32), None)
    branch, _ = lax.scan(accumulate, jnp.zeros((unit_count, D), jnp.float32), (pieces, weight_pieces))
    mean_square = lax.optimization_barrier(jnp.mean(branch * branch, axis=1, keepdims=True))
    normed = branch * lax.rsqrt(mean_square + 1e-06) * post_gain
    return residual.astype(jnp.float32) + normed
```

```python
import functools
import math

import jax
import jax.numpy as jnp
from jax import lax
from jax.experimental import pallas as pl
from jax.experimental.pallas import tpu as pltpu
from jax.sharding import PartitionSpec as P

SCALE = 168.0 ** (-0.5)
EXPONENT_SCALE = SCALE * math.log2(math.e)
EPSILON = 1e-06
AUX = 8


def split_pieces(x, count):
    pieces = []
    for _ in range(count):
        piece = x.astype(jnp.bfloat16)
        pieces.append(piece)
        x = x - piece.astype(jnp.float32)
    return pieces


def pack_aux(peak, total):
    rows = split_pieces(peak, 3) + split_pieces(total, 2)
    rows = [row.astype(jnp.float32) for row in rows]
    rows.append(jnp.zeros((AUX - len(rows), peak.shape[1]), jnp.float32))
    return jnp.concatenate(rows, axis=0).astype(jnp.bfloat16)


def unpack_aux(aux):
    aux = aux.astype(jnp.float32)
    peak = (aux[0:1] + aux[1:2]) + aux[2:3]
    total = aux[3:4] + aux[4:5]
    return peak, total


def attend_kernel(heads, head_dim, per_step, parity_ref, qa_ref, qb_ref, *refs):
    kv_refs, out_ref = refs[: 2 * per_step], refs[2 * per_step]
    for i in range(per_step):
        k_ref, v_ref = kv_refs[2 * i], kv_refs[2 * i + 1]
        width = heads * head_dim
        rows = []
        for q_ref in (qa_ref, qb_ref):
            for g in range(heads):
                rows.append(q_ref[i, :, g * head_dim : (g + 1) * head_dim])
        q = jnp.concatenate(rows, axis=0)
        scores = lax.dot_general(
            q, k_ref[0], (((1,), (1,)), ((), ())), preferred_element_type=jnp.float32
        )
        peak = jnp.max(scores, axis=1, keepdims=True)
        exponent = jnp.exp2((scores - peak) * EXPONENT_SCALE)
        total = jnp.sum(exponent, axis=1, keepdims=True)
        weighted = jnp.dot(
            exponent.astype(jnp.bfloat16), v_ref[0], preferred_element_type=jnp.float32
        )
        count = q.shape[0]
        out_ref[i, 0:head_dim, :] = weighted.T.astype(jnp.bfloat16)
        lane = lax.broadcasted_iota(jnp.int32, (count, 128), 1)
        stats = jnp.where(lane == 0, peak, total).T
        out_ref[i, head_dim : head_dim + AUX, :] = pack_aux(stats[0:1], stats[1:2])


def attend(parity, qa, qb, keys, values, own_heads, per_step):
    kv_heads, positions, head_dim = keys.shape
    units = qa.shape[0]
    head_count = qa.shape[1] // head_dim
    group = head_count // kv_heads
    heads = min(group, own_heads)
    per_device = own_heads // heads
    tasks = head_count // (2 * heads)
    rows = 2 * units * heads

    def first_head(t, parity):
        return (2 * (t // per_device) + parity) * own_heads + (t % per_device) * heads

    def kv_spec(i):
        return pl.BlockSpec(
            (1, positions, head_dim),
            lambda s, parity: (first_head(s * per_step + i, parity[0]) // group, 0, 0),
        )

    def pick(q):
        q = q.reshape(units, head_count // (2 * own_heads), 2, per_device, heads * head_dim)
        q = lax.dynamic_index_in_dim(q, parity, axis=2, keepdims=False)
        return q.reshape(units, tasks, heads * head_dim).transpose(1, 0, 2)

    q_spec = pl.BlockSpec((per_step, units, heads * head_dim), lambda s, parity: (s, 0, 0))
    operands, specs = [], []
    for i in range(per_step):
        operands += [keys, values]
        specs += [kv_spec(i), kv_spec(i)]
    return pl.pallas_call(
        functools.partial(attend_kernel, heads, head_dim, per_step),
        out_shape=jax.ShapeDtypeStruct((tasks, head_dim + AUX, rows), jnp.bfloat16),
        grid_spec=pltpu.PrefetchScalarGridSpec(
            num_scalar_prefetch=1,
            grid=(tasks // per_step,),
            in_specs=[q_spec, q_spec] + specs,
            out_specs=pl.BlockSpec(
                (per_step, head_dim + AUX, rows), lambda s, parity: (s, 0, 0)
            ),
        ),
        cost_estimate=pl.CostEstimate(
            flops=4 * tasks * rows * positions * head_dim,
            bytes_accessed=4 * tasks * positions * head_dim,
            transcendentals=tasks * rows * positions,
        ),
    )(parity.reshape(1), pick(qa), pick(qb), *operands)


def combine_kernel(head_dim, a_ref, b_ref, out_ref):
    for t in range(a_ref.shape[0]):
        peak_a, total_a = unpack_aux(a_ref[t, head_dim : head_dim + AUX, :])
        peak_b, total_b = unpack_aux(b_ref[t, head_dim : head_dim + AUX, :])
        peak = jnp.maximum(peak_a, peak_b)
        scale_a = jnp.exp2((peak_a - peak) * EXPONENT_SCALE)
        scale_b = jnp.exp2((peak_b - peak) * EXPONENT_SCALE)
        weighted = (
            a_ref[t, 0:head_dim, :].astype(jnp.float32) * scale_a
            + b_ref[t, 0:head_dim, :].astype(jnp.float32) * scale_b
        )
        out_ref[t, 0:head_dim, :] = weighted.astype(jnp.bfloat16)
        out_ref[t, head_dim : head_dim + AUX, :] = pack_aux(
            peak, total_a * scale_a + total_b * scale_b
        )


def project_kernel(heads, head_dim, part_ref, weight_ref, own_ref, other_ref, lhs_ref):
    chips, per_device, _, rows = part_ref.shape
    units = rows // (2 * heads)

    @pl.when(pl.program_id(0) == 0)
    def _():
        for j in range(per_device):
            stats = [
                unpack_aux(part_ref[p, j, head_dim : head_dim + AUX, :]) for p in range(chips)
            ]
            peak = functools.reduce(jnp.maximum, [s[0] for s in stats])
            total = jnp.zeros((1, rows), jnp.float32)
            weighted = jnp.zeros((head_dim, rows), jnp.float32)
            for p in range(chips):
                scale = jnp.exp2((stats[p][0] - peak) * EXPONENT_SCALE)
                total += stats[p][1] * scale
                weighted += part_ref[p, j, 0:head_dim, :].astype(jnp.float32) * scale
            attended = (weighted / total).T.astype(jnp.bfloat16)
            for side in range(2):
                for g in range(heads):
                    start = (side * heads + g) * units
                    column = (j * heads + g) * head_dim
                    lhs_ref[side * units : (side + 1) * units, column : column + head_dim] = (
                        attended[start : start + units]
                    )

    out = jnp.dot(lhs_ref[...], weight_ref[...], preferred_element_type=jnp.float32)
    out = out.astype(jnp.bfloat16)
    own_ref[...] = out[0:units]
    other_ref[...] = out[units : 2 * units]


def project(parts, out_weight, heads, head_dim):
    own_width, width = out_weight.shape
    chips, per_device, _, rows = parts.shape
    units = rows // (2 * heads)
    tile = next(t for t in (768, 640, 512, 384, 256, 128, width) if width % t == 0)
    shape = jax.ShapeDtypeStruct((units, width), jnp.bfloat16)
    return pl.pallas_call(
        functools.partial(project_kernel, heads, head_dim),
        out_shape=(shape, shape),
        grid=(width // tile,),
        in_specs=[
            pl.BlockSpec(parts.shape, lambda c: (0, 0, 0, 0)),
            pl.BlockSpec((own_width, tile), lambda c: (0, c)),
        ],
        out_specs=(
            pl.BlockSpec((units, tile), lambda c: (0, c)),
            pl.BlockSpec((units, tile), lambda c: (0, c)),
        ),
        scratch_shapes=[pltpu.VMEM((2 * units, own_width), jnp.bfloat16)],
    )(parts, out_weight)


def finish_kernel(terms_ref, residual_ref, gain_ref, out_ref):
    branch = terms_ref[0].astype(jnp.float32)
    for p in range(1, terms_ref.shape[0]):
        branch += terms_ref[p].astype(jnp.float32)
    mean_square = jnp.mean(branch * branch, axis=1, keepdims=True)
    normed = branch * lax.rsqrt(mean_square + EPSILON) * gain_ref[...]
    out_ref[...] = residual_ref[...].astype(jnp.float32) + normed


def shards(n, queries, keys, values, residual, post_gain, out_weight):
    kv_heads, positions, head_dim = keys.shape
    chips = n // 2
    head_count = queries.shape[1] // head_dim
    own_heads = out_weight.shape[0] // head_dim
    heads = min(head_count // kv_heads, own_heads)
    per_device = own_heads // heads
    width = out_weight.shape[1]
    parity = lax.rem(lax.axis_index("ctx"), 2)
    same_core = [[2 * p + c for p in range(chips)] for c in range(2)]
    partner = [(i, i ^ 1) for i in range(n)]

    def exchange(x):
        return lax.all_to_all(x, "ctx", 0, 0, axis_index_groups=same_core)

    def swap(x):
        return lax.ppermute(x, "ctx", partner)

    own_units = queries.shape[0]
    qa = exchange(jnp.broadcast_to(queries[None], (chips,) + queries.shape))
    qa = qa.reshape(chips * own_units, queries.shape[1])
    qb = swap(qa)
    per_step = 2
    theirs = swap(attend(1 - parity, qb, qa, keys, values, own_heads, per_step))
    mine = attend(parity, qa, qb, keys, values, own_heads, per_step)
    pair = pl.pallas_call(
        functools.partial(combine_kernel, head_dim),
        out_shape=jax.ShapeDtypeStruct(mine.shape, jnp.bfloat16),
    )(mine, theirs)
    parts = exchange(pair.reshape((chips, per_device) + pair.shape[1:]))
    own_term, other_term = project(parts, out_weight, heads, head_dim)
    term = own_term.astype(jnp.float32) + swap(other_term).astype(jnp.float32)
    terms = exchange(term.astype(jnp.bfloat16).reshape(chips, own_units, width))
    return pl.pallas_call(
        finish_kernel, out_shape=jax.ShapeDtypeStruct((own_units, width), jnp.float32)
    )(terms, residual, post_gain.reshape(1, width))


def solution(mesh):
    in_specs = (
        P(("groups", "ctx"), None),
        P(None, ("groups", "ctx"), None),
        P(None, ("groups", "ctx"), None),
        P(("groups", "ctx"), None),
        P(),
        P("ctx", None),
    )
    out_specs = P(("groups", "ctx"), None)
    return jax.shard_map(
        functools.partial(shards, mesh.shape["ctx"]),
        mesh=mesh,
        in_specs=in_specs,
        out_specs=out_specs,
        check_vma=False,
    )
```

```python
import functools
import math

import jax
import jax.numpy as jnp
from jax import lax
from jax.experimental import pallas as pl
from jax.experimental.pallas import tpu as pltpu
from jax.sharding import PartitionSpec as P

SCALE = 168.0 ** (-0.5)
EXPONENT_SCALE = SCALE * math.log2(math.e)
EPSILON = 1e-06
AUX = 8
CHUNK = 2048
VMEM_SPEC = pl.BlockSpec(memory_space=pltpu.VMEM)


def params(limit=8 << 20):
    return pltpu.CompilerParams(vmem_limit_bytes=limit)


def split_pieces(x, count):
    pieces = []
    for _ in range(count):
        piece = x.astype(jnp.bfloat16)
        pieces.append(piece)
        x = x - piece.astype(jnp.float32)
    return pieces


def pack_aux(peak, total):
    rows = split_pieces(peak, 3) + split_pieces(total, 2)
    rows = [row.astype(jnp.float32) for row in rows]
    rows.append(jnp.zeros((AUX - len(rows), peak.shape[1]), jnp.float32))
    return jnp.concatenate(rows, axis=0).astype(jnp.bfloat16)


def unpack_aux(aux):
    aux = aux.astype(jnp.float32)
    peak = (aux[0:1] + aux[1:2]) + aux[2:3]
    total = aux[3:4] + aux[4:5]
    return peak, total


def spread_kernel(query_ref, out_ref):
    for p in range(out_ref.shape[0]):
        out_ref[p] = query_ref[...]


def spread(queries, copies, cover):
    return pl.pallas_call(
        spread_kernel,
        out_shape=jax.ShapeDtypeStruct((copies,) + queries.shape, queries.dtype),
        in_specs=[VMEM_SPEC],
        out_specs=VMEM_SPEC,
        compiler_params=params(2 << 20),
        cost_estimate=pl.CostEstimate(flops=cover, bytes_accessed=0, transcendentals=0),
    )(queries)


def attend_kernel(
    swapped, own_heads, heads, head_dim, chunk, tasks,
    qa_ref, qb_ref, k_ref, v_ref, out_ref, score_a, score_b,
):
    positions = k_ref.shape[1]
    group = qa_ref.shape[2] // head_dim // k_ref.shape[0]
    per_device = own_heads // heads
    parity = lax.rem(lax.axis_index("ctx"), 2)
    if swapped:
        parity, qa_ref, qb_ref = 1 - parity, qb_ref, qa_ref

    def first_head(t):
        device = 2 * (t // per_device) + parity
        return device * own_heads + (t % per_device) * heads

    def load_query(t):
        first = first_head(t)
        rows = []
        for q_ref in (qa_ref, qb_ref):
            for g in range(heads):
                start = pl.multiple_of((first + g) * head_dim, head_dim)
                for p in range(q_ref.shape[0]):
                    rows.append(q_ref[p, :, pl.ds(start, head_dim)].astype(jnp.float32))
        return jnp.concatenate(rows, axis=0).astype(jnp.bfloat16)

    def score(q, kv, start, score_ref):
        part = lax.dot_general(
            q,
            k_ref[kv, start : start + chunk, :],
            (((1,), (1,)), ((), ())),
            preferred_element_type=jnp.float32,
        )
        score_ref[:, start : start + chunk] = part
        tiles = [part[:, i : i + 128] for i in range(0, chunk, 128)]
        return functools.reduce(jnp.maximum, tiles)

    def weigh(kv, peak, start, score_ref):
        exponent = jnp.exp2((score_ref[:, start : start + chunk] - peak) * EXPONENT_SCALE)
        tiles = [exponent[:, i : i + 128] for i in range(0, chunk, 128)]
        weighted = jnp.dot(
            exponent.astype(jnp.bfloat16),
            v_ref[kv, start : start + chunk, :],
            preferred_element_type=jnp.float32,
        )
        return functools.reduce(jnp.add, tiles), weighted

    def section(t, peak, current_ref, following, next_ref):
        kv = first_head(t) // group
        if following is not None:
            q, next_kv = load_query(following), first_head(following) // group
        highest = total = weighted = None
        for start in range(0, positions, chunk):
            if following is not None:
                part = score(q, next_kv, start, next_ref)
                highest = part if highest is None else jnp.maximum(highest, part)
            exponents, product = weigh(kv, peak, start, current_ref)
            total = exponents if total is None else total + exponents
            weighted = product if weighted is None else weighted + product
        total = jnp.sum(total, axis=1, keepdims=True)
        out_ref[t, 0:head_dim, :] = weighted.T.astype(jnp.bfloat16)
        lane = lax.broadcasted_iota(jnp.int32, (peak.shape[0], 128), 1)
        stats = jnp.where(lane == 0, peak, total).T
        out_ref[t, head_dim : head_dim + AUX, :] = pack_aux(stats[0:1], stats[1:2])
        return None if highest is None else jnp.max(highest, axis=1, keepdims=True)

    q = load_query(0)
    highest = None
    for start in range(0, positions, chunk):
        part = score(q, first_head(0) // group, start, score_a)
        highest = part if highest is None else jnp.maximum(highest, part)
    peak = jnp.max(highest, axis=1, keepdims=True)

    for t in range(tasks):
        score_refs = (score_a, score_b) if t % 2 == 0 else (score_b, score_a)
        peak = section(t, peak, score_refs[0], t + 1 if t + 1 < tasks else None, score_refs[1])


def attend(swapped, qa, qb, keys, values, own_heads):
    kv_heads, positions, head_dim = keys.shape
    units = qa.shape[0] * qa.shape[1]
    head_count = qa.shape[2] // head_dim
    heads = min(head_count // kv_heads, own_heads)
    tasks = head_count // (2 * heads)
    rows = 2 * units * heads
    return pl.pallas_call(
        functools.partial(
            attend_kernel, swapped, own_heads, heads, head_dim, min(CHUNK, positions), tasks
        ),
        out_shape=jax.ShapeDtypeStruct((tasks, head_dim + AUX, rows), jnp.bfloat16),
        in_specs=[VMEM_SPEC] * 4,
        out_specs=VMEM_SPEC,
        scratch_shapes=[pltpu.VMEM((rows, positions), jnp.float32)] * 2,
        compiler_params=params(20 << 20),
        cost_estimate=pl.CostEstimate(
            flops=4 * tasks * rows * positions * head_dim,
            bytes_accessed=4 * tasks * positions * head_dim,
            transcendentals=tasks * rows * positions,
        ),
    )(qa, qb, keys, values)


def combine_kernel(head_dim, a_ref, b_ref, out_ref):
    for t in range(a_ref.shape[0]):
        peak_a, total_a = unpack_aux(a_ref[t, head_dim : head_dim + AUX, :])
        peak_b, total_b = unpack_aux(b_ref[t, head_dim : head_dim + AUX, :])
        peak = jnp.maximum(peak_a, peak_b)
        scale_a = jnp.exp2((peak_a - peak) * EXPONENT_SCALE)
        scale_b = jnp.exp2((peak_b - peak) * EXPONENT_SCALE)
        weighted = (
            a_ref[t, 0:head_dim, :].astype(jnp.float32) * scale_a
            + b_ref[t, 0:head_dim, :].astype(jnp.float32) * scale_b
        )
        out_ref[t, 0:head_dim, :] = weighted.astype(jnp.bfloat16)
        out_ref[t, head_dim : head_dim + AUX, :] = pack_aux(
            peak, total_a * scale_a + total_b * scale_b
        )


def project_kernel(heads, head_dim, tile, part_ref, weight_ref, own_ref, other_ref, lhs_ref):
    chips, per_device, _, rows = part_ref.shape
    units = rows // (2 * heads)
    for j in range(per_device):
        stats = [unpack_aux(part_ref[p, j, head_dim : head_dim + AUX, :]) for p in range(chips)]
        peak = functools.reduce(jnp.maximum, [s[0] for s in stats])
        scales = [jnp.exp2((s[0] - peak) * EXPONENT_SCALE) for s in stats]
        total = functools.reduce(jnp.add, [s[1] * x for s, x in zip(stats, scales)])
        weighted = jnp.zeros((head_dim, rows), jnp.float32)
        for p in range(chips):
            weighted += part_ref[p, j, 0:head_dim, :].astype(jnp.float32) * scales[p]
        attended = (weighted / total).T.astype(jnp.bfloat16)
        for side in range(2):
            for g in range(heads):
                start = (side * heads + g) * units
                column = (j * heads + g) * head_dim
                lhs_ref[side * units : (side + 1) * units, column : column + head_dim] = (
                    attended[start : start + units]
                )
    lhs = lhs_ref[...]
    for start in range(0, weight_ref.shape[1], tile):
        columns = slice(start, start + tile)
        out = jnp.dot(lhs, weight_ref[:, columns], preferred_element_type=jnp.float32)
        out = out.astype(jnp.bfloat16)
        own_ref[:, columns] = out[0:units]
        other_ref[:, columns] = out[units : 2 * units]


def project(parts, out_weight, heads, head_dim):
    own_width, width = out_weight.shape
    rows = parts.shape[3]
    units = rows // (2 * heads)
    tile = next(t for t in (768, 640, 512, 384, 256, 128, width) if width % t == 0)
    shape = jax.ShapeDtypeStruct((units, width), jnp.bfloat16)
    return pl.pallas_call(
        functools.partial(project_kernel, heads, head_dim, tile),
        out_shape=(shape, shape),
        in_specs=[VMEM_SPEC] * 2,
        out_specs=(VMEM_SPEC, VMEM_SPEC),
        scratch_shapes=[pltpu.VMEM((2 * units, own_width), jnp.bfloat16)],
        compiler_params=params(),
    )(parts, out_weight)


def add_kernel(own_ref, theirs_ref, out_ref):
    chips, units, _ = out_ref.shape
    term = own_ref[...].astype(jnp.float32) + theirs_ref[...].astype(jnp.float32)
    for p in range(chips):
        out_ref[p] = term[p * units : (p + 1) * units].astype(jnp.bfloat16)


def finish_kernel(terms_ref, residual_ref, gain_ref, out_ref):
    branch = terms_ref[0].astype(jnp.float32)
    for p in range(1, terms_ref.shape[0]):
        branch += terms_ref[p].astype(jnp.float32)
    mean_square = jnp.mean(branch * branch, axis=1, keepdims=True)
    normed = branch * lax.rsqrt(mean_square + EPSILON) * gain_ref[...]
    out_ref[...] = residual_ref[...].astype(jnp.float32) + normed


def shards(n, queries, keys, values, residual, post_gain, out_weight):
    kv_heads, positions, head_dim = keys.shape
    chips = n // 2
    head_count = queries.shape[1] // head_dim
    own_heads = out_weight.shape[0] // head_dim
    heads = min(head_count // kv_heads, own_heads)
    per_device = own_heads // heads
    width = out_weight.shape[1]
    same_core = [[2 * p + c for p in range(chips)] for c in range(2)]
    partner = [(i, i ^ 1) for i in range(n)]

    def exchange(x):
        return lax.all_to_all(x, "ctx", 0, 0, axis_index_groups=same_core)

    def swap(x):
        return lax.ppermute(x, "ctx", partner)

    own_units = queries.shape[0]
    cover = 4000 * keys.size * keys.dtype.itemsize
    qa = exchange(spread(queries, chips, cover))
    qb = swap(qa)
    theirs = swap(attend(True, qa, qb, keys, values, own_heads))
    mine = attend(False, qa, qb, keys, values, own_heads)
    pair = pl.pallas_call(
        functools.partial(combine_kernel, head_dim),
        out_shape=jax.ShapeDtypeStruct(mine.shape, jnp.bfloat16),
        in_specs=[VMEM_SPEC] * 2,
        out_specs=VMEM_SPEC,
        compiler_params=params(),
    )(mine, theirs)
    parts = exchange(pair.reshape((chips, per_device) + pair.shape[1:]))
    own_term, other_term = project(parts, out_weight, heads, head_dim)
    term = pl.pallas_call(
        add_kernel,
        out_shape=jax.ShapeDtypeStruct((chips, own_units, width), jnp.bfloat16),
        in_specs=[VMEM_SPEC] * 2,
        out_specs=VMEM_SPEC,
        compiler_params=params(),
    )(own_term, swap(other_term))
    return pl.pallas_call(
        finish_kernel,
        out_shape=jax.ShapeDtypeStruct((own_units, width), jnp.float32),
        in_specs=[VMEM_SPEC] * 3,
        out_specs=VMEM_SPEC,
        compiler_params=params(),
    )(exchange(term), residual, post_gain.reshape(1, width))


def solution(mesh):
    in_specs = (
        P(("groups", "ctx"), None),
        P(None, ("groups", "ctx"), None),
        P(None, ("groups", "ctx"), None),
        P(("groups", "ctx"), None),
        P(),
        P("ctx", None),
    )
    out_specs = P(("groups", "ctx"), None)
    return jax.shard_map(
        functools.partial(shards, mesh.shape["ctx"]),
        mesh=mesh,
        in_specs=in_specs,
        out_specs=out_specs,
        check_vma=False,
    )
```

```python
import functools
import math

import jax
import jax.numpy as jnp
from jax import lax
from jax.experimental import pallas as pl
from jax.experimental.pallas import tpu as pltpu
from jax.sharding import PartitionSpec as P

SCALE = 168.0 ** (-0.5)
EXPONENT_SCALE = SCALE * math.log2(math.e)
EPSILON = 1e-06
AUX = 8
CHUNK = 2048
VMEM_SPEC = pl.BlockSpec(memory_space=pltpu.VMEM)


def params(limit=8 << 20):
    return pltpu.CompilerParams(vmem_limit_bytes=limit)


def split_pieces(x, count):
    pieces = []
    for _ in range(count):
        piece = x.astype(jnp.bfloat16)
        pieces.append(piece)
        x = x - piece.astype(jnp.float32)
    return pieces


def pack_aux(peak, total):
    rows = split_pieces(peak, 3) + split_pieces(total, 2)
    rows = [row.astype(jnp.float32) for row in rows]
    rows.append(jnp.zeros((AUX - len(rows), peak.shape[1]), jnp.float32))
    return jnp.concatenate(rows, axis=0).astype(jnp.bfloat16)


def unpack_aux(aux):
    aux = aux.astype(jnp.float32)
    peak = (aux[0:1] + aux[1:2]) + aux[2:3]
    total = aux[3:4] + aux[4:5]
    return peak, total


def spread_kernel(query_ref, out_ref):
    for p in range(out_ref.shape[0]):
        out_ref[p] = query_ref[...]


def spread(queries, copies, cover):
    return pl.pallas_call(
        spread_kernel,
        out_shape=jax.ShapeDtypeStruct((copies,) + queries.shape, queries.dtype),
        in_specs=[VMEM_SPEC],
        out_specs=VMEM_SPEC,
        compiler_params=params(2 << 20),
        cost_estimate=pl.CostEstimate(flops=cover, bytes_accessed=0, transcendentals=0),
    )(queries)


def attend_kernel(
    swapped, own_heads, heads, head_dim, chunk, tasks,
    qa_ref, qb_ref, k_ref, v_ref, out_ref, score_a, score_b,
):
    positions = k_ref.shape[1]
    group = qa_ref.shape[2] // head_dim // k_ref.shape[0]
    per_device = own_heads // heads
    parity = lax.rem(lax.axis_index("ctx"), 2)
    if swapped:
        parity, qa_ref, qb_ref = 1 - parity, qb_ref, qa_ref

    def first_head(t):
        device = 2 * (t // per_device) + parity
        return device * own_heads + (t % per_device) * heads

    def load_query(t):
        first = first_head(t)
        rows = []
        for q_ref in (qa_ref, qb_ref):
            for g in range(heads):
                start = pl.multiple_of((first + g) * head_dim, head_dim)
                for p in range(q_ref.shape[0]):
                    rows.append(q_ref[p, :, pl.ds(start, head_dim)].astype(jnp.float32))
        return jnp.concatenate(rows, axis=0).astype(jnp.bfloat16)

    def score(q, kv, start, score_ref):
        part = lax.dot_general(
            q,
            k_ref[kv, start : start + chunk, :],
            (((1,), (1,)), ((), ())),
            preferred_element_type=jnp.float32,
        )
        score_ref[:, start : start + chunk] = part
        tiles = [part[:, i : i + 128] for i in range(0, chunk, 128)]
        return functools.reduce(jnp.maximum, tiles)

    def weigh(kv, peak, start, score_ref):
        exponent = jnp.exp2((score_ref[:, start : start + chunk] - peak) * EXPONENT_SCALE)
        tiles = [exponent[:, i : i + 128] for i in range(0, chunk, 128)]
        weighted = jnp.dot(
            exponent.astype(jnp.bfloat16),
            v_ref[kv, start : start + chunk, :],
            preferred_element_type=jnp.float32,
        )
        return functools.reduce(jnp.add, tiles), weighted

    def section(t, peak, current_ref, following, next_ref):
        kv = first_head(t) // group
        if following is not None:
            q, next_kv = load_query(following), first_head(following) // group
        highest = total = weighted = None
        for start in range(0, positions, chunk):
            if following is not None:
                part = score(q, next_kv, start, next_ref)
                highest = part if highest is None else jnp.maximum(highest, part)
            exponents, product = weigh(kv, peak, start, current_ref)
            total = exponents if total is None else total + exponents
            weighted = product if weighted is None else weighted + product
        total = jnp.sum(total, axis=1, keepdims=True)
        out_ref[t, 0:head_dim, :] = weighted.T.astype(jnp.bfloat16)
        lane = lax.broadcasted_iota(jnp.int32, (peak.shape[0], 128), 1)
        stats = jnp.where(lane == 0, peak, total).T
        out_ref[t, head_dim : head_dim + AUX, :] = pack_aux(stats[0:1], stats[1:2])
        return None if highest is None else jnp.max(highest, axis=1, keepdims=True)

    q = load_query(0)
    highest = None
    for start in range(0, positions, chunk):
        part = score(q, first_head(0) // group, start, score_a)
        highest = part if highest is None else jnp.maximum(highest, part)
    peak = jnp.max(highest, axis=1, keepdims=True)

    for t in range(tasks):
        score_refs = (score_a, score_b) if t % 2 == 0 else (score_b, score_a)
        peak = section(t, peak, score_refs[0], t + 1 if t + 1 < tasks else None, score_refs[1])


def attend(swapped, qa, qb, keys, values, own_heads):
    kv_heads, positions, head_dim = keys.shape
    units = qa.shape[0] * qa.shape[1]
    head_count = qa.shape[2] // head_dim
    heads = min(head_count // kv_heads, own_heads)
    tasks = head_count // (2 * heads)
    rows = 2 * units * heads
    return pl.pallas_call(
        functools.partial(
            attend_kernel, swapped, own_heads, heads, head_dim, min(CHUNK, positions), tasks
        ),
        out_shape=jax.ShapeDtypeStruct((tasks, head_dim + AUX, rows), jnp.bfloat16),
        in_specs=[VMEM_SPEC] * 4,
        out_specs=VMEM_SPEC,
        scratch_shapes=[pltpu.VMEM((rows, positions), jnp.float32)] * 2,
        compiler_params=params(20 << 20),
        cost_estimate=pl.CostEstimate(
            flops=4 * tasks * rows * positions * head_dim,
            bytes_accessed=4 * tasks * positions * head_dim,
            transcendentals=tasks * rows * positions,
        ),
    )(qa, qb, keys, values)


def combine_kernel(head_dim, a_ref, b_ref, out_ref):
    for t in range(a_ref.shape[0]):
        peak_a, total_a = unpack_aux(a_ref[t, head_dim : head_dim + AUX, :])
        peak_b, total_b = unpack_aux(b_ref[t, head_dim : head_dim + AUX, :])
        peak = jnp.maximum(peak_a, peak_b)
        scale_a = jnp.exp2((peak_a - peak) * EXPONENT_SCALE)
        scale_b = jnp.exp2((peak_b - peak) * EXPONENT_SCALE)
        weighted = (
            a_ref[t, 0:head_dim, :].astype(jnp.float32) * scale_a
            + b_ref[t, 0:head_dim, :].astype(jnp.float32) * scale_b
        )
        out_ref[t, 0:head_dim, :] = weighted.astype(jnp.bfloat16)
        out_ref[t, head_dim : head_dim + AUX, :] = pack_aux(
            peak, total_a * scale_a + total_b * scale_b
        )


def project_kernel(heads, head_dim, tile, part_ref, weight_ref, own_ref, other_ref, lhs_ref):
    chips, per_device, _, rows = part_ref.shape
    units = rows // (2 * heads)
    for j in range(per_device):
        stats = [unpack_aux(part_ref[p, j, head_dim : head_dim + AUX, :]) for p in range(chips)]
        peak = functools.reduce(jnp.maximum, [s[0] for s in stats])
        scales = [jnp.exp2((s[0] - peak) * EXPONENT_SCALE) for s in stats]
        total = functools.reduce(jnp.add, [s[1] * x for s, x in zip(stats, scales)])
        weighted = jnp.zeros((head_dim, rows), jnp.float32)
        for p in range(chips):
            weighted += part_ref[p, j, 0:head_dim, :].astype(jnp.float32) * scales[p]
        attended = (weighted / total).T.astype(jnp.bfloat16)
        for side in range(2):
            for g in range(heads):
                start = (side * heads + g) * units
                column = (j * heads + g) * head_dim
                lhs_ref[side * units : (side + 1) * units, column : column + head_dim] = (
                    attended[start : start + units]
                )
    lhs = lhs_ref[...]
    for start in range(0, weight_ref.shape[1], tile):
        columns = slice(start, start + tile)
        out = jnp.dot(lhs, weight_ref[:, columns], preferred_element_type=jnp.float32)
        out = out.astype(jnp.bfloat16)
        own_ref[:, columns] = out[0:units]
        other_ref[:, columns] = out[units : 2 * units]


def project(parts, out_weight, heads, head_dim):
    own_width, width = out_weight.shape
    rows = parts.shape[3]
    units = rows // (2 * heads)
    tile = next(t for t in (768, 640, 512, 384, 256, 128, width) if width % t == 0)
    shape = jax.ShapeDtypeStruct((units, width), jnp.bfloat16)
    return pl.pallas_call(
        functools.partial(project_kernel, heads, head_dim, tile),
        out_shape=(shape, shape),
        in_specs=[VMEM_SPEC] * 2,
        out_specs=(VMEM_SPEC, VMEM_SPEC),
        scratch_shapes=[pltpu.VMEM((2 * units, own_width), jnp.bfloat16)],
        compiler_params=params(),
    )(parts, out_weight)


def add_kernel(own_ref, theirs_ref, out_ref):
    chips, units, _ = out_ref.shape
    term = own_ref[...].astype(jnp.float32) + theirs_ref[...].astype(jnp.float32)
    for p in range(chips):
        out_ref[p] = term[p * units : (p + 1) * units].astype(jnp.bfloat16)


def finish_kernel(terms_ref, residual_ref, gain_ref, out_ref):
    branch = terms_ref[0].astype(jnp.float32)
    for p in range(1, terms_ref.shape[0]):
        branch += terms_ref[p].astype(jnp.float32)
    mean_square = jnp.mean(branch * branch, axis=1, keepdims=True)
    normed = branch * lax.rsqrt(mean_square + EPSILON) * gain_ref[...][None]
    out_ref[...] = residual_ref[...].astype(jnp.float32) + normed


def shards(n, queries, keys, values, residual, post_gain, out_weight):
    kv_heads, positions, head_dim = keys.shape
    chips = n // 2
    head_count = queries.shape[1] // head_dim
    own_heads = out_weight.shape[0] // head_dim
    heads = min(head_count // kv_heads, own_heads)
    per_device = own_heads // heads
    width = out_weight.shape[1]
    same_core = [[2 * p + c for p in range(chips)] for c in range(2)]
    partner = [(i, i ^ 1) for i in range(n)]

    def exchange(x):
        return lax.all_to_all(x, "ctx", 0, 0, axis_index_groups=same_core)

    def swap(x):
        return lax.ppermute(x, "ctx", partner)

    own_units = queries.shape[0]
    cover = 4000 * keys.size * keys.dtype.itemsize
    qa = exchange(spread(queries, chips, cover))
    qb = swap(qa)
    theirs = swap(attend(True, qa, qb, keys, values, own_heads))
    mine = attend(False, qa, qb, keys, values, own_heads)
    pair = pl.pallas_call(
        functools.partial(combine_kernel, head_dim),
        out_shape=jax.ShapeDtypeStruct(mine.shape, jnp.bfloat16),
        in_specs=[VMEM_SPEC] * 2,
        out_specs=VMEM_SPEC,
        compiler_params=params(),
    )(mine, theirs)
    parts = exchange(pair.reshape((chips, per_device) + pair.shape[1:]))
    own_term, other_term = project(parts, out_weight, heads, head_dim)
    term = pl.pallas_call(
        add_kernel,
        out_shape=jax.ShapeDtypeStruct((chips, own_units, width), jnp.bfloat16),
        in_specs=[VMEM_SPEC] * 2,
        out_specs=VMEM_SPEC,
        compiler_params=params(),
    )(own_term, swap(other_term))
    return pl.pallas_call(
        finish_kernel,
        out_shape=jax.ShapeDtypeStruct((own_units, width), jnp.float32),
        in_specs=[VMEM_SPEC] * 3,
        out_specs=VMEM_SPEC,
        compiler_params=params(),
    )(exchange(term), residual, post_gain)


def solution(mesh):
    in_specs = (
        P(("groups", "ctx"), None),
        P(None, ("groups", "ctx"), None),
        P(None, ("groups", "ctx"), None),
        P(("groups", "ctx"), None),
        P(),
        P("ctx", None),
    )
    out_specs = P(("groups", "ctx"), None)
    return jax.shard_map(
        functools.partial(shards, mesh.shape["ctx"]),
        mesh=mesh,
        in_specs=in_specs,
        out_specs=out_specs,
        check_vma=False,
    )
```

```python
import functools
import math

import jax
import jax.numpy as jnp
from jax import lax
from jax.experimental import pallas as pl
from jax.experimental.pallas import tpu as pltpu
from jax.sharding import PartitionSpec as P

SCALE = 168.0 ** (-0.5)
EXPONENT_SCALE = SCALE * math.log2(math.e)
EPSILON = 1e-06
AUX = 8
CHUNK = 2048
VMEM_SPEC = pl.BlockSpec(memory_space=pltpu.VMEM)


def params(limit=8 << 20):
    return pltpu.CompilerParams(vmem_limit_bytes=limit)


def split_pieces(x, count):
    pieces = []
    for _ in range(count):
        piece = x.astype(jnp.bfloat16)
        pieces.append(piece)
        x = x - piece.astype(jnp.float32)
    return pieces


def pack_aux(peak, total):
    rows = split_pieces(peak, 3) + split_pieces(total, 2)
    rows = [row.astype(jnp.float32) for row in rows]
    rows.append(jnp.zeros((AUX - len(rows), peak.shape[1]), jnp.float32))
    return jnp.concatenate(rows, axis=0).astype(jnp.bfloat16)


def unpack_aux(aux):
    aux = aux.astype(jnp.float32)
    peak = (aux[0:1] + aux[1:2]) + aux[2:3]
    total = aux[3:4] + aux[4:5]
    return peak, total


def core_parity(swapped):
    parity = lax.rem(lax.axis_index("ctx"), 2)
    return 1 - parity if swapped else parity


def fetch_kernel(in_ref, out_ref, sem):
    copy = pltpu.make_async_copy(in_ref, out_ref, sem)
    copy.start()
    copy.wait()


def fetch(x):
    return pl.pallas_call(
        fetch_kernel,
        out_shape=jax.ShapeDtypeStruct(x.shape, x.dtype),
        in_specs=[pl.BlockSpec(memory_space=pltpu.HBM)],
        out_specs=VMEM_SPEC,
        scratch_shapes=[pltpu.SemaphoreType.DMA],
        compiler_params=params(2 << 20),
        cost_estimate=pl.CostEstimate(
            flops=0, bytes_accessed=64 * x.size * x.dtype.itemsize, transcendentals=0
        ),
    )(pltpu.with_memory_space_constraint(x, pltpu.HBM))


def spread_kernel(own_width, own_ref, partner_ref, out_ref):
    chips, units, _ = out_ref.shape
    parity = core_parity(False)
    for p in range(chips):
        start = pl.multiple_of((2 * p + 1 - parity) * own_width, own_width)
        own = own_ref[:, pl.ds(start, own_width)].astype(jnp.float32)
        partner = partner_ref[:, pl.ds(start, own_width)].astype(jnp.float32)
        first, second = (
            jnp.where(parity == 0, own, partner),
            jnp.where(parity == 0, partner, own),
        )
        block = jnp.concatenate([first, second], axis=0).astype(jnp.bfloat16)
        for q in range(chips):
            out_ref[q, :, p * own_width : (p + 1) * own_width] = block


def spread(queries, partner_queries, chips, own_width, cover):
    return pl.pallas_call(
        functools.partial(spread_kernel, own_width),
        out_shape=jax.ShapeDtypeStruct(
            (chips, 2 * queries.shape[0], chips * own_width), queries.dtype
        ),
        in_specs=[VMEM_SPEC] * 2,
        out_specs=VMEM_SPEC,
        compiler_params=params(2 << 20),
        cost_estimate=pl.CostEstimate(flops=cover, bytes_accessed=0, transcendentals=0),
    )(queries, partner_queries)


def attend_kernel(
    swapped, own_heads, heads, group, head_dim, chunk, tasks,
    q_ref, k_ref, v_ref, out_ref, score_a, score_b,
):
    positions = k_ref.shape[1]
    per_device = own_heads // heads
    parity = core_parity(swapped)

    def first_head(t):
        device = 2 * (t // per_device) + parity
        return device * own_heads + (t % per_device) * heads

    def load_query(t):
        first = t * heads
        rows = [
            q_ref[:, (first + g) * head_dim : (first + g + 1) * head_dim] for g in range(heads)
        ]
        return jnp.concatenate(rows, axis=0)

    def score(q, kv, start, score_ref):
        part = lax.dot_general(
            q,
            k_ref[kv, start : start + chunk, :],
            (((1,), (1,)), ((), ())),
            preferred_element_type=jnp.float32,
        )
        score_ref[:, start : start + chunk] = part
        tiles = [part[:, i : i + 128] for i in range(0, chunk, 128)]
        return functools.reduce(jnp.maximum, tiles)

    def weigh(kv, peak, start, score_ref):
        exponent = jnp.exp2((score_ref[:, start : start + chunk] - peak) * EXPONENT_SCALE)
        tiles = [exponent[:, i : i + 128] for i in range(0, chunk, 128)]
        weighted = jnp.dot(
            exponent.astype(jnp.bfloat16),
            v_ref[kv, start : start + chunk, :],
            preferred_element_type=jnp.float32,
        )
        return functools.reduce(jnp.add, tiles), weighted

    def section(t, peak, current_ref, following, next_ref):
        kv = first_head(t) // group
        if following is not None:
            q, next_kv = load_query(following), first_head(following) // group
        highest = total = weighted = None
        for start in range(0, positions, chunk):
            if following is not None:
                part = score(q, next_kv, start, next_ref)
                highest = part if highest is None else jnp.maximum(highest, part)
            exponents, product = weigh(kv, peak, start, current_ref)
            total = exponents if total is None else total + exponents
            weighted = product if weighted is None else weighted + product
        total = jnp.sum(total, axis=1, keepdims=True)
        out_ref[t, 0:head_dim, :] = weighted.T.astype(jnp.bfloat16)
        lane = lax.broadcasted_iota(jnp.int32, (peak.shape[0], 128), 1)
        stats = jnp.where(lane == 0, peak, total).T
        out_ref[t, head_dim : head_dim + AUX, :] = pack_aux(stats[0:1], stats[1:2])
        return None if highest is None else jnp.max(highest, axis=1, keepdims=True)

    q = load_query(0)
    highest = None
    for start in range(0, positions, chunk):
        part = score(q, first_head(0) // group, start, score_a)
        highest = part if highest is None else jnp.maximum(highest, part)
    peak = jnp.max(highest, axis=1, keepdims=True)

    for t in range(tasks):
        score_refs = (score_a, score_b) if t % 2 == 0 else (score_b, score_a)
        peak = section(t, peak, score_refs[0], t + 1 if t + 1 < tasks else None, score_refs[1])


def attend(swapped, queries, keys, values, own_heads, head_count):
    kv_heads, positions, head_dim = keys.shape
    units = queries.shape[0]
    group = head_count // kv_heads
    heads = min(group, own_heads)
    tasks = head_count // (2 * heads)
    rows = units * heads
    return pl.pallas_call(
        functools.partial(
            attend_kernel, swapped, own_heads, heads, group, head_dim, min(CHUNK, positions), tasks
        ),
        out_shape=jax.ShapeDtypeStruct((tasks, head_dim + AUX, rows), jnp.bfloat16),
        in_specs=[VMEM_SPEC] * 3,
        out_specs=VMEM_SPEC,
        scratch_shapes=[pltpu.VMEM((rows, positions), jnp.float32)] * 2,
        compiler_params=params(20 << 20),
        cost_estimate=pl.CostEstimate(
            flops=4 * tasks * rows * positions * head_dim,
            bytes_accessed=4 * tasks * positions * head_dim,
            transcendentals=tasks * rows * positions,
        ),
    )(queries, keys, values)


def combine_kernel(head_dim, a_ref, b_ref, out_ref):
    for t in range(a_ref.shape[0]):
        peak_a, total_a = unpack_aux(a_ref[t, head_dim : head_dim + AUX, :])
        peak_b, total_b = unpack_aux(b_ref[t, head_dim : head_dim + AUX, :])
        peak = jnp.maximum(peak_a, peak_b)
        scale_a = jnp.exp2((peak_a - peak) * EXPONENT_SCALE)
        scale_b = jnp.exp2((peak_b - peak) * EXPONENT_SCALE)
        weighted = (
            a_ref[t, 0:head_dim, :].astype(jnp.float32) * scale_a
            + b_ref[t, 0:head_dim, :].astype(jnp.float32) * scale_b
        )
        out_ref[t, 0:head_dim, :] = weighted.astype(jnp.bfloat16)
        out_ref[t, head_dim : head_dim + AUX, :] = pack_aux(
            peak, total_a * scale_a + total_b * scale_b
        )


def project_kernel(heads, head_dim, tile, part_ref, weight_ref, own_ref, other_ref, lhs_ref):
    chips, per_device, _, rows = part_ref.shape
    units = rows // (2 * heads)
    few = units // chips
    parity = core_parity(False)
    for j in range(per_device):
        stats = [unpack_aux(part_ref[p, j, head_dim : head_dim + AUX, :]) for p in range(chips)]
        peak = functools.reduce(jnp.maximum, [s[0] for s in stats])
        scales = [jnp.exp2((s[0] - peak) * EXPONENT_SCALE) for s in stats]
        total = functools.reduce(jnp.add, [s[1] * x for s, x in zip(stats, scales)])
        weighted = jnp.zeros((head_dim, rows), jnp.float32)
        for p in range(chips):
            weighted += part_ref[p, j, 0:head_dim, :].astype(jnp.float32) * scales[p]
        attended = (weighted / total).T
        for g in range(heads):
            column = (j * heads + g) * head_dim
            sides = [[], []]
            for p in range(chips):
                start = (g * chips + p) * 2 * few
                pair = attended[start : start + few], attended[start + few : start + 2 * few]
                sides[0].append(jnp.where(parity == 0, pair[0], pair[1]))
                sides[1].append(jnp.where(parity == 0, pair[1], pair[0]))
            side = jnp.concatenate(sides[0] + sides[1], axis=0)
            lhs_ref[:, column : column + head_dim] = side.astype(jnp.bfloat16)
    lhs = lhs_ref[...]
    for start in range(0, weight_ref.shape[1], tile):
        columns = slice(start, start + tile)
        out = jnp.dot(lhs, weight_ref[:, columns], preferred_element_type=jnp.float32)
        out = out.astype(jnp.bfloat16)
        own_ref[:, columns] = out[0:units]
        other_ref[:, columns] = out[units : 2 * units]


def project(parts, out_weight, heads, head_dim):
    own_width, width = out_weight.shape
    rows = parts.shape[3]
    units = rows // (2 * heads)
    tile = next(t for t in (768, 640, 512, 384, 256, 128, width) if width % t == 0)
    shape = jax.ShapeDtypeStruct((units, width), jnp.bfloat16)
    return pl.pallas_call(
        functools.partial(project_kernel, heads, head_dim, tile),
        out_shape=(shape, shape),
        in_specs=[VMEM_SPEC] * 2,
        out_specs=(VMEM_SPEC, VMEM_SPEC),
        scratch_shapes=[pltpu.VMEM((2 * units, own_width), jnp.bfloat16)],
        compiler_params=params(),
    )(parts, out_weight)


def add_kernel(own_ref, theirs_ref, out_ref):
    chips, units, _ = out_ref.shape
    term = own_ref[...].astype(jnp.float32) + theirs_ref[...].astype(jnp.float32)
    for p in range(chips):
        out_ref[p] = term[p * units : (p + 1) * units].astype(jnp.bfloat16)


def finish_kernel(terms_ref, residual_ref, gain_ref, out_ref):
    branch = terms_ref[0].astype(jnp.float32)
    for p in range(1, terms_ref.shape[0]):
        branch += terms_ref[p].astype(jnp.float32)
    mean_square = jnp.mean(branch * branch, axis=1, keepdims=True)
    normed = branch * lax.rsqrt(mean_square + EPSILON) * gain_ref[...][None]
    out_ref[...] = residual_ref[...].astype(jnp.float32) + normed


def shards(n, queries, keys, values, residual, post_gain, out_weight):
    kv_heads, positions, head_dim = keys.shape
    chips = n // 2
    head_count = queries.shape[1] // head_dim
    own_heads = out_weight.shape[0] // head_dim
    heads = min(head_count // kv_heads, own_heads)
    per_device = own_heads // heads
    width = out_weight.shape[1]
    same_core = [[2 * p + c for p in range(chips)] for c in range(2)]
    partner = [(i, i ^ 1) for i in range(n)]

    def exchange(x):
        return lax.all_to_all(x, "ctx", 0, 0, axis_index_groups=same_core)

    def swap(x):
        return lax.ppermute(x, "ctx", partner)

    own_units = queries.shape[0]
    cover = 4000 * keys.size * keys.dtype.itemsize
    first = exchange(spread(fetch(queries), swap(queries), chips, out_weight.shape[0], cover))
    first = first.reshape(2 * chips * own_units, first.shape[2])
    second = swap(first)
    theirs = swap(attend(True, first, keys, values, own_heads, head_count))
    mine = attend(False, second, keys, values, own_heads, head_count)
    pair = pl.pallas_call(
        functools.partial(combine_kernel, head_dim),
        out_shape=jax.ShapeDtypeStruct(mine.shape, jnp.bfloat16),
        in_specs=[VMEM_SPEC] * 2,
        out_specs=VMEM_SPEC,
        compiler_params=params(),
    )(mine, theirs)
    parts = exchange(pair.reshape((chips, per_device) + pair.shape[1:]))
    own_term, other_term = project(parts, out_weight, heads, head_dim)
    term = pl.pallas_call(
        add_kernel,
        out_shape=jax.ShapeDtypeStruct((chips, own_units, width), jnp.bfloat16),
        in_specs=[VMEM_SPEC] * 2,
        out_specs=VMEM_SPEC,
        compiler_params=params(),
    )(own_term, swap(other_term))
    return pl.pallas_call(
        finish_kernel,
        out_shape=jax.ShapeDtypeStruct((own_units, width), jnp.float32),
        in_specs=[VMEM_SPEC] * 3,
        out_specs=VMEM_SPEC,
        compiler_params=params(),
    )(exchange(term), residual, post_gain)


def solution(mesh):
    in_specs = (
        P(("groups", "ctx"), None),
        P(None, ("groups", "ctx"), None),
        P(None, ("groups", "ctx"), None),
        P(("groups", "ctx"), None),
        P(),
        P("ctx", None),
    )
    out_specs = P(("groups", "ctx"), None)
    return jax.shard_map(
        functools.partial(shards, mesh.shape["ctx"]),
        mesh=mesh,
        in_specs=in_specs,
        out_specs=out_specs,
        check_vma=False,
    )
```

```python
import functools
import math

import jax
import jax.numpy as jnp
from jax import lax
from jax.experimental import pallas as pl
from jax.experimental.pallas import tpu as pltpu
from jax.sharding import PartitionSpec as P

SCALE = 168.0 ** (-0.5)
EXPONENT_SCALE = SCALE * math.log2(math.e)
EPSILON = 1e-06
AUX = 8
CHUNK = 2048
VMEM_SPEC = pl.BlockSpec(memory_space=pltpu.VMEM)


def params(limit=8 << 20):
    return pltpu.CompilerParams(vmem_limit_bytes=limit)


def split_pieces(x, count):
    pieces = []
    for _ in range(count):
        piece = x.astype(jnp.bfloat16)
        pieces.append(piece)
        x = x - piece.astype(jnp.float32)
    return pieces


def pack_aux(peak, total):
    rows = split_pieces(peak, 3) + split_pieces(total, 2)
    rows = [row.astype(jnp.float32) for row in rows]
    rows.append(jnp.zeros((AUX - len(rows), peak.shape[1]), jnp.float32))
    return jnp.concatenate(rows, axis=0).astype(jnp.bfloat16)


def unpack_aux(aux):
    aux = aux.astype(jnp.float32)
    peak = (aux[0:1] + aux[1:2]) + aux[2:3]
    total = aux[3:4] + aux[4:5]
    return peak, total


def slot_of(offset):
    return lax.bitwise_xor(lax.rem(lax.axis_index("ctx"), 4), offset)


def fetch_kernel(in_ref, out_ref, sem):
    copy = pltpu.make_async_copy(in_ref, out_ref, sem)
    copy.start()
    copy.wait()


def fetch(x):
    return pl.pallas_call(
        fetch_kernel,
        out_shape=jax.ShapeDtypeStruct(x.shape, x.dtype),
        in_specs=[pl.BlockSpec(memory_space=pltpu.HBM)],
        out_specs=VMEM_SPEC,
        scratch_shapes=[pltpu.SemaphoreType.DMA],
        compiler_params=params(2 << 20),
        cost_estimate=pl.CostEstimate(
            flops=0, bytes_accessed=64 * x.size * x.dtype.itemsize, transcendentals=0
        ),
    )(pltpu.with_memory_space_constraint(x, pltpu.HBM))


def spread_kernel(own_width, *refs):
    query_refs, out_ref = refs[:4], refs[4]
    planes = out_ref.shape[0]
    own, wanted = slot_of(0), slot_of(3)
    for z in range(planes):
        start = pl.multiple_of((4 * z + wanted) * own_width, own_width)
        blocks = [ref[:, pl.ds(start, own_width)].astype(jnp.float32) for ref in query_refs]
        rows = []
        for slot in range(4):
            row = blocks[slot]
            for other in range(1, 4):
                row = jnp.where(own == other, blocks[slot ^ other], row)
            rows.append(row)
        block = jnp.concatenate(rows, axis=0).astype(jnp.bfloat16)
        for q in range(planes):
            out_ref[q, :, z * own_width : (z + 1) * own_width] = block


def spread(queries, planes, own_width, cover):
    return pl.pallas_call(
        functools.partial(spread_kernel, own_width),
        out_shape=jax.ShapeDtypeStruct(
            (planes, 4 * queries[0].shape[0], planes * own_width), queries[0].dtype
        ),
        in_specs=[VMEM_SPEC] * 4,
        out_specs=VMEM_SPEC,
        compiler_params=params(2 << 20),
        cost_estimate=pl.CostEstimate(flops=cover, bytes_accessed=0, transcendentals=0),
    )(*queries)


def attend_kernel(
    offset, own_heads, heads, group, head_dim, chunk, tasks,
    q_ref, k_ref, v_ref, *refs,
):
    out_ref, score_a, score_b = refs[-3:]
    positions = k_ref.shape[1]
    per_device = own_heads // heads
    slot = slot_of(offset)

    def first_head(t):
        device = 4 * (t // per_device) + slot
        return device * own_heads + (t % per_device) * heads

    def load_query(t):
        first = t * heads
        rows = [
            q_ref[:, (first + g) * head_dim : (first + g + 1) * head_dim] for g in range(heads)
        ]
        return jnp.concatenate(rows, axis=0)

    def score(q, kv, start, score_ref):
        part = lax.dot_general(
            q,
            k_ref[kv, start : start + chunk, :],
            (((1,), (1,)), ((), ())),
            preferred_element_type=jnp.float32,
        )
        score_ref[:, start : start + chunk] = part
        tiles = [part[:, i : i + 128] for i in range(0, chunk, 128)]
        return functools.reduce(jnp.maximum, tiles)

    def weigh(kv, peak, start, score_ref):
        exponent = jnp.exp2((score_ref[:, start : start + chunk] - peak) * EXPONENT_SCALE)
        tiles = [exponent[:, i : i + 128] for i in range(0, chunk, 128)]
        weighted = jnp.dot(
            exponent.astype(jnp.bfloat16),
            v_ref[kv, start : start + chunk, :],
            preferred_element_type=jnp.float32,
        )
        return functools.reduce(jnp.add, tiles), weighted

    def section(t, peak, current_ref, following, next_ref):
        kv = first_head(t) // group
        if following is not None:
            q, next_kv = load_query(following), first_head(following) // group
        highest = total = weighted = None
        for start in range(0, positions, chunk):
            if following is not None:
                part = score(q, next_kv, start, next_ref)
                highest = part if highest is None else jnp.maximum(highest, part)
            exponents, product = weigh(kv, peak, start, current_ref)
            total = exponents if total is None else total + exponents
            weighted = product if weighted is None else weighted + product
        total = jnp.sum(total, axis=1, keepdims=True)
        out_ref[t, 0:head_dim, :] = weighted.T.astype(jnp.bfloat16)
        lane = lax.broadcasted_iota(jnp.int32, (peak.shape[0], 128), 1)
        stats = jnp.where(lane == 0, peak, total).T
        out_ref[t, head_dim : head_dim + AUX, :] = pack_aux(stats[0:1], stats[1:2])
        return None if highest is None else jnp.max(highest, axis=1, keepdims=True)

    q = load_query(0)
    highest = None
    for start in range(0, positions, chunk):
        part = score(q, first_head(0) // group, start, score_a)
        highest = part if highest is None else jnp.maximum(highest, part)
    peak = jnp.max(highest, axis=1, keepdims=True)

    for t in range(tasks):
        score_refs = (score_a, score_b) if t % 2 == 0 else (score_b, score_a)
        peak = section(t, peak, score_refs[0], t + 1 if t + 1 < tasks else None, score_refs[1])


def attend(offset, queries, keys, values, own_heads, head_count, after):
    kv_heads, positions, head_dim = keys.shape
    units = queries.shape[0]
    group = head_count // kv_heads
    heads = min(group, own_heads)
    tasks = head_count // (4 * heads)
    rows = units * heads
    return pl.pallas_call(
        functools.partial(
            attend_kernel, offset, own_heads, heads, group, head_dim, min(CHUNK, positions), tasks
        ),
        out_shape=jax.ShapeDtypeStruct((tasks, head_dim + AUX, rows), jnp.bfloat16),
        in_specs=[VMEM_SPEC] * (3 + len(after)),
        out_specs=VMEM_SPEC,
        scratch_shapes=[pltpu.VMEM((rows, positions), jnp.float32)] * 2,
        compiler_params=params(20 << 20),
        cost_estimate=pl.CostEstimate(
            flops=4 * tasks * rows * positions * head_dim,
            bytes_accessed=4 * tasks * positions * head_dim,
            transcendentals=tasks * rows * positions,
        ),
    )(queries, keys, values, *after)


def join(head_dim, parts):
    stats = [unpack_aux(part[head_dim : head_dim + AUX, :]) for part in parts]
    peak = functools.reduce(jnp.maximum, [s[0] for s in stats])
    scales = [jnp.exp2((s[0] - peak) * EXPONENT_SCALE) for s in stats]
    total = functools.reduce(jnp.add, [s[1] * x for s, x in zip(stats, scales)])
    weighted = [
        part[0:head_dim, :].astype(jnp.float32) * x for part, x in zip(parts, scales)
    ]
    return peak, total, functools.reduce(jnp.add, weighted)


def combine_kernel(head_dim, *refs):
    out_ref = refs[-1]
    for t in range(out_ref.shape[0]):
        peak, total, weighted = join(head_dim, [ref.at[t] for ref in refs[:-1]])
        out_ref[t, 0:head_dim, :] = weighted.astype(jnp.bfloat16)
        out_ref[t, head_dim : head_dim + AUX, :] = pack_aux(peak, total)


def combine(head_dim, *parts):
    return pl.pallas_call(
        functools.partial(combine_kernel, head_dim),
        out_shape=jax.ShapeDtypeStruct(parts[0].shape, jnp.bfloat16),
        in_specs=[VMEM_SPEC] * len(parts),
        out_specs=VMEM_SPEC,
        compiler_params=params(),
    )(*parts)


def project_kernel(chips, heads, head_dim, tile, part_ref, weight_ref, own_ref, other_ref, lhs_ref):
    planes, per_device, _, rows = part_ref.shape
    units = rows // (2 * heads)
    few = units // chips
    parity = lax.rem(lax.axis_index("ctx"), 2)
    for j in range(per_device):
        _, total, weighted = join(head_dim, [part_ref.at[z, j] for z in range(planes)])
        attended = (weighted / total).T
        for g in range(heads):
            column = (j * heads + g) * head_dim
            sides = [[], []]
            for p in range(chips):
                start = (g * chips + p) * 2 * few
                pair = attended[start : start + few], attended[start + few : start + 2 * few]
                sides[0].append(jnp.where(parity == 0, pair[0], pair[1]))
                sides[1].append(jnp.where(parity == 0, pair[1], pair[0]))
            side = jnp.concatenate(sides[0] + sides[1], axis=0)
            lhs_ref[:, column : column + head_dim] = side.astype(jnp.bfloat16)
    lhs = lhs_ref[...]
    for start in range(0, weight_ref.shape[1], tile):
        columns = slice(start, start + tile)
        out = jnp.dot(lhs, weight_ref[:, columns], preferred_element_type=jnp.float32)
        out = out.astype(jnp.bfloat16)
        own_ref[:, columns] = out[0:units]
        other_ref[:, columns] = out[units : 2 * units]


def project(parts, out_weight, chips, heads, head_dim):
    own_width, width = out_weight.shape
    rows = parts.shape[3]
    units = rows // (2 * heads)
    tile = next(t for t in (768, 640, 512, 384, 256, 128, width) if width % t == 0)
    shape = jax.ShapeDtypeStruct((units, width), jnp.bfloat16)
    return pl.pallas_call(
        functools.partial(project_kernel, chips, heads, head_dim, tile),
        out_shape=(shape, shape),
        in_specs=[VMEM_SPEC] * 2,
        out_specs=(VMEM_SPEC, VMEM_SPEC),
        scratch_shapes=[pltpu.VMEM((2 * units, own_width), jnp.bfloat16)],
        compiler_params=params(),
    )(parts, out_weight)


def add_kernel(own_ref, theirs_ref, out_ref):
    chips, units, _ = out_ref.shape
    term = own_ref[...].astype(jnp.float32) + theirs_ref[...].astype(jnp.float32)
    for p in range(chips):
        out_ref[p] = term[p * units : (p + 1) * units].astype(jnp.bfloat16)


def finish_kernel(terms_ref, residual_ref, gain_ref, out_ref):
    branch = terms_ref[0].astype(jnp.float32)
    for p in range(1, terms_ref.shape[0]):
        branch += terms_ref[p].astype(jnp.float32)
    mean_square = jnp.mean(branch * branch, axis=1, keepdims=True)
    normed = branch * lax.rsqrt(mean_square + EPSILON) * gain_ref[...][None]
    out_ref[...] = residual_ref[...].astype(jnp.float32) + normed


def shards(n, queries, keys, values, residual, post_gain, out_weight):
    kv_heads, positions, head_dim = keys.shape
    chips = n // 2
    head_count = queries.shape[1] // head_dim
    own_heads = out_weight.shape[0] // head_dim
    heads = min(head_count // kv_heads, own_heads)
    per_device = own_heads // heads
    width = out_weight.shape[1]
    planes = n // 4
    same_core = [[2 * p + c for p in range(chips)] for c in range(2)]
    same_slot = [[4 * z + slot for z in range(planes)] for slot in range(4)]

    def exchange(x, groups):
        return lax.all_to_all(x, "ctx", 0, 0, axis_index_groups=groups)

    def swap(x, offset):
        return lax.ppermute(x, "ctx", [(i, i ^ offset) for i in range(n)])

    def attended(offset, x, *after):
        return attend(offset, x, keys, values, own_heads, head_count, after)

    own_units = queries.shape[0]
    cover = 4000 * keys.size * keys.dtype.itemsize
    plane = [fetch(queries)] + [swap(queries, offset) for offset in (1, 2, 3)]
    first = exchange(spread(plane, planes, out_weight.shape[0], cover), same_slot)
    first = first.reshape(n * own_units, first.shape[2])
    second, third = swap(first, 1), swap(first, 2)
    fourth = swap(third, 1)
    pair = swap(attended(3, first), 1)
    joined = combine(head_dim, attended(2, second), pair)
    across = swap(joined, 2)
    beside = swap(attended(1, third, joined), 1)
    own = combine(head_dim, attended(0, fourth), beside, across)
    parts = exchange(own.reshape((planes, per_device) + own.shape[1:]), same_slot)
    own_term, other_term = project(parts, out_weight, chips, heads, head_dim)
    term = pl.pallas_call(
        add_kernel,
        out_shape=jax.ShapeDtypeStruct((chips, own_units, width), jnp.bfloat16),
        in_specs=[VMEM_SPEC] * 2,
        out_specs=VMEM_SPEC,
        compiler_params=params(),
    )(own_term, swap(other_term, 1))
    return pl.pallas_call(
        finish_kernel,
        out_shape=jax.ShapeDtypeStruct((own_units, width), jnp.float32),
        in_specs=[VMEM_SPEC] * 3,
        out_specs=VMEM_SPEC,
        compiler_params=params(),
    )(exchange(term, same_core), residual, post_gain)


def solution(mesh):
    in_specs = (
        P(("groups", "ctx"), None),
        P(None, ("groups", "ctx"), None),
        P(None, ("groups", "ctx"), None),
        P(("groups", "ctx"), None),
        P(),
        P("ctx", None),
    )
    out_specs = P(("groups", "ctx"), None)
    return jax.shard_map(
        functools.partial(shards, mesh.shape["ctx"]),
        mesh=mesh,
        in_specs=in_specs,
        out_specs=out_specs,
        check_vma=False,
    )
```

```python
import functools
import math

import jax
import jax.numpy as jnp
from jax import lax
from jax.experimental import pallas as pl
from jax.experimental.pallas import tpu as pltpu
from jax.sharding import PartitionSpec as P


SCALE = 168.0 ** (-0.5)
EXPONENT_SCALE = SCALE * math.log2(math.e)
EPSILON = 1e-06
AUX = 8
CHUNK = 2048
VMEM_SPEC = pl.BlockSpec(memory_space=pltpu.VMEM)


def params(limit=8 << 20):
    return pltpu.CompilerParams(vmem_limit_bytes=limit)


def split_pieces(x, count):
    pieces = []
    for _ in range(count):
        piece = x.astype(jnp.bfloat16)
        pieces.append(piece)
        x = x - piece.astype(jnp.float32)
    return pieces


def pack_aux(peak, total):
    rows = split_pieces(peak, 3) + split_pieces(total, 2)
    rows = [row.astype(jnp.float32) for row in rows]
    rows.append(jnp.zeros((AUX - len(rows), peak.shape[1]), jnp.float32))
    return jnp.concatenate(rows, axis=0).astype(jnp.bfloat16)


def unpack_aux(aux):
    aux = aux.astype(jnp.float32)
    peak = (aux[0:1] + aux[1:2]) + aux[2:3]
    total = aux[3:4] + aux[4:5]
    return peak, total


def slot_of(offset):
    return lax.bitwise_xor(lax.rem(lax.axis_index("ctx"), 4), offset)


def fetch_kernel(in_ref, out_ref, sem):
    copy = pltpu.make_async_copy(in_ref, out_ref, sem)
    copy.start()
    copy.wait()


def fetch(x):
    return pl.pallas_call(
        fetch_kernel,
        out_shape=jax.ShapeDtypeStruct(x.shape, x.dtype),
        in_specs=[pl.BlockSpec(memory_space=pltpu.HBM)],
        out_specs=VMEM_SPEC,
        scratch_shapes=[pltpu.SemaphoreType.DMA],
        compiler_params=params(2 << 20),
        cost_estimate=pl.CostEstimate(
            flops=0, bytes_accessed=64 * x.size * x.dtype.itemsize, transcendentals=0
        ),
    )(pltpu.with_memory_space_constraint(x, pltpu.HBM))


def spread_kernel(own_width, own_ref, partner_ref, out_ref):
    chips = out_ref.shape[0]
    slot = slot_of(1)
    parity = lax.rem(slot, 2)
    for p in range(chips):
        start = pl.multiple_of((2 * p + parity) * own_width, own_width)
        own = own_ref[:, pl.ds(start, own_width)].astype(jnp.float32)
        partner = partner_ref[:, pl.ds(start, own_width)].astype(jnp.float32)
        first = jnp.where(parity == 1, own, partner)
        second = jnp.where(parity == 1, partner, own)
        block = jnp.concatenate([first, second], axis=0).astype(jnp.bfloat16)
        for q in range(chips):
            place = p // 2 + (chips // 2 if p % 2 == q % 2 else 0)
            out_ref[q, :, place * own_width : (place + 1) * own_width] = block


def spread(queries, partner_queries, chips, own_width, cover):
    return pl.pallas_call(
        functools.partial(spread_kernel, own_width),
        out_shape=jax.ShapeDtypeStruct(
            (chips, 2 * queries.shape[0], chips * own_width), queries.dtype
        ),
        in_specs=[VMEM_SPEC] * 2,
        out_specs=VMEM_SPEC,
        compiler_params=params(2 << 20),
        cost_estimate=pl.CostEstimate(flops=cover, bytes_accessed=0, transcendentals=0),
    )(queries, partner_queries)


def attend_kernel(
    offset, own_heads, heads, group, head_dim, chunk, tasks,
    q_ref, k_ref, v_ref, *refs,
):
    out_ref, score_a, score_b = refs[-3:]
    positions = k_ref.shape[1]
    per_device = own_heads // heads
    slot = slot_of(offset)

    def first_head(t):
        device = 4 * (t // per_device) + slot
        return device * own_heads + (t % per_device) * heads

    def load_query(t):
        first = t * heads + (0 if offset >= 2 else tasks * heads)
        rows = [
            q_ref[:, (first + g) * head_dim : (first + g + 1) * head_dim] for g in range(heads)
        ]
        return jnp.concatenate(rows, axis=0)

    def score(q, kv, start, score_ref):
        part = lax.dot_general(
            q,
            k_ref[kv, start : start + chunk, :],
            (((1,), (1,)), ((), ())),
            preferred_element_type=jnp.float32,
        )
        score_ref[:, start : start + chunk] = part
        tiles = [part[:, i : i + 128] for i in range(0, chunk, 128)]
        return functools.reduce(jnp.maximum, tiles)

    def weigh(kv, peak, start, score_ref):
        exponent = jnp.exp2((score_ref[:, start : start + chunk] - peak) * EXPONENT_SCALE)
        tiles = [exponent[:, i : i + 128] for i in range(0, chunk, 128)]
        weighted = jnp.dot(
            exponent.astype(jnp.bfloat16),
            v_ref[kv, start : start + chunk, :],
            preferred_element_type=jnp.float32,
        )
        return functools.reduce(jnp.add, tiles), weighted

    def section(t, peak, current_ref, following, next_ref):
        kv = first_head(t) // group
        if following is not None:
            q, next_kv = load_query(following), first_head(following) // group
        highest = total = weighted = None
        for start in range(0, positions, chunk):
            if following is not None:
                part = score(q, next_kv, start, next_ref)
                highest = part if highest is None else jnp.maximum(highest, part)
            exponents, product = weigh(kv, peak, start, current_ref)
            total = exponents if total is None else total + exponents
            weighted = product if weighted is None else weighted + product
        total = jnp.sum(total, axis=1, keepdims=True)
        out_ref[t, 0:head_dim, :] = weighted.T.astype(jnp.bfloat16)
        lane = lax.broadcasted_iota(jnp.int32, (peak.shape[0], 128), 1)
        stats = jnp.where(lane == 0, peak, total).T
        out_ref[t, head_dim : head_dim + AUX, :] = pack_aux(stats[0:1], stats[1:2])
        return None if highest is None else jnp.max(highest, axis=1, keepdims=True)

    q = load_query(0)
    highest = None
    for start in range(0, positions, chunk):
        part = score(q, first_head(0) // group, start, score_a)
        highest = part if highest is None else jnp.maximum(highest, part)
    peak = jnp.max(highest, axis=1, keepdims=True)

    for t in range(tasks):
        score_refs = (score_a, score_b) if t % 2 == 0 else (score_b, score_a)
        peak = section(t, peak, score_refs[0], t + 1 if t + 1 < tasks else None, score_refs[1])


def attend(offset, queries, keys, values, own_heads, head_count, after):
    kv_heads, positions, head_dim = keys.shape
    units = queries.shape[0]
    group = head_count // kv_heads
    heads = min(group, own_heads)
    tasks = head_count // (4 * heads)
    rows = units * heads
    return pl.pallas_call(
        functools.partial(
            attend_kernel, offset, own_heads, heads, group, head_dim, min(CHUNK, positions), tasks
        ),
        out_shape=jax.ShapeDtypeStruct((tasks, head_dim + AUX, rows), jnp.bfloat16),
        in_specs=[VMEM_SPEC] * (3 + len(after)),
        out_specs=VMEM_SPEC,
        scratch_shapes=[pltpu.VMEM((rows, positions), jnp.float32)] * 2,
        compiler_params=params(20 << 20),
        cost_estimate=pl.CostEstimate(
            flops=4 * tasks * rows * positions * head_dim,
            bytes_accessed=4 * tasks * positions * head_dim,
            transcendentals=tasks * rows * positions,
        ),
    )(queries, keys, values, *after)


def join(head_dim, parts):
    stats = [unpack_aux(part[head_dim : head_dim + AUX, :]) for part in parts]
    peak = functools.reduce(jnp.maximum, [s[0] for s in stats])
    scales = [jnp.exp2((s[0] - peak) * EXPONENT_SCALE) for s in stats]
    total = functools.reduce(jnp.add, [s[1] * x for s, x in zip(stats, scales)])
    weighted = [
        part[0:head_dim, :].astype(jnp.float32) * x for part, x in zip(parts, scales)
    ]
    return peak, total, functools.reduce(jnp.add, weighted)


def combine_kernel(head_dim, *refs):
    out_ref = refs[-1]
    for t in range(out_ref.shape[0]):
        peak, total, weighted = join(head_dim, [ref.at[t] for ref in refs[:-1]])
        out_ref[t, 0:head_dim, :] = weighted.astype(jnp.bfloat16)
        out_ref[t, head_dim : head_dim + AUX, :] = pack_aux(peak, total)


def combine(head_dim, *parts):
    return pl.pallas_call(
        functools.partial(combine_kernel, head_dim),
        out_shape=jax.ShapeDtypeStruct(parts[0].shape, jnp.bfloat16),
        in_specs=[VMEM_SPEC] * len(parts),
        out_specs=VMEM_SPEC,
        compiler_params=params(),
    )(*parts)


def project_kernel(chips, heads, head_dim, tile, part_ref, weight_ref, own_ref, other_ref, lhs_ref):
    planes, per_device, _, rows = part_ref.shape
    units = rows // (2 * heads)
    few = units // chips
    parity = lax.rem(lax.axis_index("ctx"), 2)
    for j in range(per_device):
        _, total, weighted = join(head_dim, [part_ref.at[z, j] for z in range(planes)])
        attended = (weighted / total).T
        for g in range(heads):
            column = (j * heads + g) * head_dim
            sides = [[], []]
            for p in range(chips):
                start = (g * chips + p) * 2 * few
                pair = attended[start : start + few], attended[start + few : start + 2 * few]
                sides[0].append(jnp.where(parity == 0, pair[0], pair[1]))
                sides[1].append(jnp.where(parity == 0, pair[1], pair[0]))
            side = jnp.concatenate(sides[0] + sides[1], axis=0)
            lhs_ref[:, column : column + head_dim] = side.astype(jnp.bfloat16)
    lhs = lhs_ref[...]
    for start in range(0, weight_ref.shape[1], tile):
        columns = slice(start, start + tile)
        out = jnp.dot(lhs, weight_ref[:, columns], preferred_element_type=jnp.float32)
        out = out.astype(jnp.bfloat16)
        own_ref[:, columns] = out[0:units]
        other_ref[:, columns] = out[units : 2 * units]


def project(parts, out_weight, chips, heads, head_dim):
    own_width, width = out_weight.shape
    rows = parts.shape[3]
    units = rows // (2 * heads)
    tile = next(t for t in (768, 640, 512, 384, 256, 128, width) if width % t == 0)
    shape = jax.ShapeDtypeStruct((units, width), jnp.bfloat16)
    return pl.pallas_call(
        functools.partial(project_kernel, chips, heads, head_dim, tile),
        out_shape=(shape, shape),
        in_specs=[VMEM_SPEC] * 2,
        out_specs=(VMEM_SPEC, VMEM_SPEC),
        scratch_shapes=[pltpu.VMEM((2 * units, own_width), jnp.bfloat16)],
        compiler_params=params(),
    )(parts, out_weight)


def add_kernel(own_ref, theirs_ref, out_ref):
    chips, units, _ = out_ref.shape
    term = own_ref[...].astype(jnp.float32) + theirs_ref[...].astype(jnp.float32)
    for p in range(chips):
        out_ref[p] = term[p * units : (p + 1) * units].astype(jnp.bfloat16)


def finish_kernel(terms_ref, residual_ref, gain_ref, out_ref):
    branch = terms_ref[0].astype(jnp.float32)
    for p in range(1, terms_ref.shape[0]):
        branch += terms_ref[p].astype(jnp.float32)
    mean_square = jnp.mean(branch * branch, axis=1, keepdims=True)
    normed = branch * lax.rsqrt(mean_square + EPSILON) * gain_ref[...][None]
    out_ref[...] = residual_ref[...].astype(jnp.float32) + normed


def sublayer(n, queries, keys, values, residual, post_gain, out_weight):
    kv_heads, _, head_dim = keys.shape
    chips = n // 2
    head_count = queries.shape[1] // head_dim
    own_heads = out_weight.shape[0] // head_dim
    heads = min(head_count // kv_heads, own_heads)
    per_device = own_heads // heads
    width = out_weight.shape[1]
    planes = n // 4
    same_core = [[2 * p + c for p in range(chips)] for c in range(2)]
    same_slot = [[4 * z + slot for z in range(planes)] for slot in range(4)]

    def exchange(x, groups):
        return lax.all_to_all(x, "ctx", 0, 0, axis_index_groups=groups)

    def swap(x, offset):
        return lax.ppermute(x, "ctx", [(i, i ^ offset) for i in range(n)])

    def attended(offset, x, *after):
        return attend(offset, x, keys, values, own_heads, head_count, after)

    own_units = queries.shape[0]
    cover = 4000 * keys.size * keys.dtype.itemsize
    ahead = spread(fetch(queries), swap(queries, 1), chips, out_weight.shape[0], cover)
    theirs = exchange(ahead, same_core)
    theirs = theirs.reshape(n * own_units, theirs.shape[2])
    mine = swap(theirs, 1)
    pair = swap(attended(3, theirs), 1)
    joined = combine(head_dim, attended(2, mine), pair)
    across = swap(joined, 2)
    beside = swap(attended(1, theirs, joined), 1)
    own = combine(head_dim, attended(0, mine, joined), beside, across)
    parts = exchange(own.reshape((planes, per_device) + own.shape[1:]), same_slot)
    own_term, other_term = project(parts, out_weight, chips, heads, head_dim)
    term = pl.pallas_call(
        add_kernel,
        out_shape=jax.ShapeDtypeStruct((chips, own_units, width), jnp.bfloat16),
        in_specs=[VMEM_SPEC] * 2,
        out_specs=VMEM_SPEC,
        compiler_params=params(),
    )(own_term, swap(other_term, 1))
    return pl.pallas_call(
        finish_kernel,
        out_shape=jax.ShapeDtypeStruct((own_units, width), jnp.float32),
        in_specs=[VMEM_SPEC] * 3,
        out_specs=VMEM_SPEC,
        compiler_params=params(),
    )(exchange(term, same_core), residual, post_gain)


def solution(mesh):
    in_specs = (
        P(("groups", "ctx"), None),
        P(None, ("groups", "ctx"), None),
        P(None, ("groups", "ctx"), None),
        P(("groups", "ctx"), None),
        P(),
        P("ctx", None),
    )
    out_specs = P(("groups", "ctx"), None)
    return jax.shard_map(
        functools.partial(sublayer, mesh.shape["ctx"]),
        mesh=mesh,
        in_specs=in_specs,
        out_specs=out_specs,
        check_vma=False,
    )
```

```python
import functools
import math

import jax
import jax.numpy as jnp
from jax import lax
from jax.experimental import pallas as pl
from jax.experimental.pallas import tpu as pltpu
from jax.sharding import PartitionSpec as P


SCALE = 168.0 ** (-0.5)
EXPONENT_SCALE = SCALE * math.log2(math.e)
EPSILON = 1e-06
AUX = 8
CHUNK = 2048
VMEM_SPEC = pl.BlockSpec(memory_space=pltpu.VMEM)


def params(limit=8 << 20):
    return pltpu.CompilerParams(vmem_limit_bytes=limit)


def split_pieces(x, count):
    pieces = []
    for _ in range(count):
        piece = x.astype(jnp.bfloat16)
        pieces.append(piece)
        x = x - piece.astype(jnp.float32)
    return pieces


def pack_aux(peak, total):
    rows = split_pieces(peak, 3) + split_pieces(total, 2)
    rows = [row.astype(jnp.float32) for row in rows]
    rows.append(jnp.zeros((AUX - len(rows), peak.shape[1]), jnp.float32))
    return jnp.concatenate(rows, axis=0).astype(jnp.bfloat16)


def unpack_aux(aux):
    aux = aux.astype(jnp.float32)
    peak = (aux[0:1] + aux[1:2]) + aux[2:3]
    total = aux[3:4] + aux[4:5]
    return peak, total


def slot_of(offset):
    return lax.bitwise_xor(lax.rem(lax.axis_index("ctx"), 4), offset)


def fetch_kernel(in_ref, out_ref, sem):
    copy = pltpu.make_async_copy(in_ref, out_ref, sem)
    copy.start()
    copy.wait()


def fetch(x):
    return pl.pallas_call(
        fetch_kernel,
        out_shape=jax.ShapeDtypeStruct(x.shape, x.dtype),
        in_specs=[pl.BlockSpec(memory_space=pltpu.HBM)],
        out_specs=VMEM_SPEC,
        scratch_shapes=[pltpu.SemaphoreType.DMA],
        compiler_params=params(2 << 20),
        cost_estimate=pl.CostEstimate(
            flops=0, bytes_accessed=64 * x.size * x.dtype.itemsize, transcendentals=0
        ),
    )(pltpu.with_memory_space_constraint(x, pltpu.HBM))


def spread_kernel(own_width, *refs):
    query_refs, out_ref = refs[:4], refs[4]
    planes = out_ref.shape[0]
    own, wanted = slot_of(0), slot_of(3)
    for z in range(planes):
        start = pl.multiple_of((4 * z + wanted) * own_width, own_width)
        blocks = [ref[:, pl.ds(start, own_width)].astype(jnp.float32) for ref in query_refs]
        rows = []
        for slot in range(4):
            row = blocks[slot]
            for other in range(1, 4):
                row = jnp.where(own == other, blocks[slot ^ other], row)
            rows.append(row)
        block = jnp.concatenate(rows, axis=0).astype(jnp.bfloat16)
        for q in range(planes):
            out_ref[q, :, z * own_width : (z + 1) * own_width] = block


def spread(queries, planes, own_width, cover):
    return pl.pallas_call(
        functools.partial(spread_kernel, own_width),
        out_shape=jax.ShapeDtypeStruct(
            (planes, 4 * queries[0].shape[0], planes * own_width), queries[0].dtype
        ),
        in_specs=[VMEM_SPEC] * 4,
        out_specs=VMEM_SPEC,
        compiler_params=params(2 << 20),
        cost_estimate=pl.CostEstimate(flops=cover, bytes_accessed=0, transcendentals=0),
    )(*queries)


def attend_kernel(
    offset, own_heads, heads, group, head_dim, chunk, tasks,
    q_ref, k_ref, v_ref, *refs,
):
    out_ref, score_a, score_b = refs[-3:]
    positions = k_ref.shape[1]
    per_device = own_heads // heads
    slot = slot_of(offset)

    def first_head(t):
        device = 4 * (t // per_device) + slot
        return device * own_heads + (t % per_device) * heads

    def load_query(t):
        first = t * heads
        rows = [
            q_ref[:, (first + g) * head_dim : (first + g + 1) * head_dim] for g in range(heads)
        ]
        return jnp.concatenate(rows, axis=0)

    def score(q, kv, start, score_ref):
        part = lax.dot_general(
            q,
            k_ref[kv, start : start + chunk, :],
            (((1,), (1,)), ((), ())),
            preferred_element_type=jnp.float32,
        )
        score_ref[:, start : start + chunk] = part
        tiles = [part[:, i : i + 128] for i in range(0, chunk, 128)]
        return functools.reduce(jnp.maximum, tiles)

    def weigh(kv, peak, start, score_ref):
        exponent = jnp.exp2((score_ref[:, start : start + chunk] - peak) * EXPONENT_SCALE)
        tiles = [exponent[:, i : i + 128] for i in range(0, chunk, 128)]
        weighted = jnp.dot(
            exponent.astype(jnp.bfloat16),
            v_ref[kv, start : start + chunk, :],
            preferred_element_type=jnp.float32,
        )
        return functools.reduce(jnp.add, tiles), weighted

    def section(t, peak, current_ref, following, next_ref):
        kv = first_head(t) // group
        if following is not None:
            q, next_kv = load_query(following), first_head(following) // group
        highest = total = weighted = None
        for start in range(0, positions, chunk):
            if following is not None:
                part = score(q, next_kv, start, next_ref)
                highest = part if highest is None else jnp.maximum(highest, part)
            exponents, product = weigh(kv, peak, start, current_ref)
            total = exponents if total is None else total + exponents
            weighted = product if weighted is None else weighted + product
        total = jnp.sum(total, axis=1, keepdims=True)
        out_ref[t, 0:head_dim, :] = weighted.T.astype(jnp.bfloat16)
        lane = lax.broadcasted_iota(jnp.int32, (peak.shape[0], 128), 1)
        stats = jnp.where(lane == 0, peak, total).T
        out_ref[t, head_dim : head_dim + AUX, :] = pack_aux(stats[0:1], stats[1:2])
        return None if highest is None else jnp.max(highest, axis=1, keepdims=True)

    q = load_query(0)
    highest = None
    for start in range(0, positions, chunk):
        part = score(q, first_head(0) // group, start, score_a)
        highest = part if highest is None else jnp.maximum(highest, part)
    peak = jnp.max(highest, axis=1, keepdims=True)

    for t in range(tasks):
        score_refs = (score_a, score_b) if t % 2 == 0 else (score_b, score_a)
        peak = section(t, peak, score_refs[0], t + 1 if t + 1 < tasks else None, score_refs[1])


def attend(offset, queries, keys, values, own_heads, head_count, after):
    kv_heads, positions, head_dim = keys.shape
    units = queries.shape[0]
    group = head_count // kv_heads
    heads = min(group, own_heads)
    tasks = head_count // (4 * heads)
    rows = units * heads
    return pl.pallas_call(
        functools.partial(
            attend_kernel, offset, own_heads, heads, group, head_dim, min(CHUNK, positions), tasks
        ),
        out_shape=jax.ShapeDtypeStruct((tasks, head_dim + AUX, rows), jnp.bfloat16),
        in_specs=[VMEM_SPEC] * (3 + len(after)),
        out_specs=VMEM_SPEC,
        scratch_shapes=[pltpu.VMEM((rows, positions), jnp.float32)] * 2,
        compiler_params=params(20 << 20),
        cost_estimate=pl.CostEstimate(
            flops=4 * tasks * rows * positions * head_dim,
            bytes_accessed=4 * tasks * positions * head_dim,
            transcendentals=tasks * rows * positions,
        ),
    )(queries, keys, values, *after)


def join(head_dim, parts):
    stats = [unpack_aux(part[head_dim : head_dim + AUX, :]) for part in parts]
    peak = functools.reduce(jnp.maximum, [s[0] for s in stats])
    scales = [jnp.exp2((s[0] - peak) * EXPONENT_SCALE) for s in stats]
    total = functools.reduce(jnp.add, [s[1] * x for s, x in zip(stats, scales)])
    weighted = [
        part[0:head_dim, :].astype(jnp.float32) * x for part, x in zip(parts, scales)
    ]
    return peak, total, functools.reduce(jnp.add, weighted)


def combine_kernel(head_dim, *refs):
    out_ref = refs[-1]
    for t in range(out_ref.shape[0]):
        peak, total, weighted = join(head_dim, [ref.at[t] for ref in refs[:-1]])
        out_ref[t, 0:head_dim, :] = weighted.astype(jnp.bfloat16)
        out_ref[t, head_dim : head_dim + AUX, :] = pack_aux(peak, total)


def combine(head_dim, *parts):
    return pl.pallas_call(
        functools.partial(combine_kernel, head_dim),
        out_shape=jax.ShapeDtypeStruct(parts[0].shape, jnp.bfloat16),
        in_specs=[VMEM_SPEC] * len(parts),
        out_specs=VMEM_SPEC,
        compiler_params=params(),
    )(*parts)


def project_kernel(chips, heads, head_dim, tile, part_ref, weight_ref, own_ref, other_ref, lhs_ref):
    planes, per_device, _, rows = part_ref.shape
    units = rows // (2 * heads)
    few = units // chips
    parity = lax.rem(lax.axis_index("ctx"), 2)
    for j in range(per_device):
        _, total, weighted = join(head_dim, [part_ref.at[z, j] for z in range(planes)])
        attended = (weighted / total).T
        for g in range(heads):
            column = (j * heads + g) * head_dim
            sides = [[], []]
            for p in range(chips):
                start = (g * chips + p) * 2 * few
                pair = attended[start : start + few], attended[start + few : start + 2 * few]
                sides[0].append(jnp.where(parity == 0, pair[0], pair[1]))
                sides[1].append(jnp.where(parity == 0, pair[1], pair[0]))
            side = jnp.concatenate(sides[0] + sides[1], axis=0)
            lhs_ref[:, column : column + head_dim] = side.astype(jnp.bfloat16)
    lhs = lhs_ref[...]
    for start in range(0, weight_ref.shape[1], tile):
        columns = slice(start, start + tile)
        out = jnp.dot(lhs, weight_ref[:, columns], preferred_element_type=jnp.float32)
        out = out.astype(jnp.bfloat16)
        own_ref[:, columns] = out[0:units]
        other_ref[:, columns] = out[units : 2 * units]


def project(parts, out_weight, chips, heads, head_dim):
    own_width, width = out_weight.shape
    rows = parts.shape[3]
    units = rows // (2 * heads)
    tile = next(t for t in (768, 640, 512, 384, 256, 128, width) if width % t == 0)
    shape = jax.ShapeDtypeStruct((units, width), jnp.bfloat16)
    return pl.pallas_call(
        functools.partial(project_kernel, chips, heads, head_dim, tile),
        out_shape=(shape, shape),
        in_specs=[VMEM_SPEC] * 2,
        out_specs=(VMEM_SPEC, VMEM_SPEC),
        scratch_shapes=[pltpu.VMEM((2 * units, own_width), jnp.bfloat16)],
        compiler_params=params(),
    )(parts, out_weight)


def add_kernel(own_ref, theirs_ref, out_ref):
    chips, units, _ = out_ref.shape
    term = own_ref[...].astype(jnp.float32) + theirs_ref[...].astype(jnp.float32)
    for p in range(chips):
        out_ref[p] = term[p * units : (p + 1) * units].astype(jnp.bfloat16)


def finish_kernel(terms_ref, residual_ref, gain_ref, out_ref):
    branch = terms_ref[0].astype(jnp.float32)
    for p in range(1, terms_ref.shape[0]):
        branch += terms_ref[p].astype(jnp.float32)
    mean_square = jnp.mean(branch * branch, axis=1, keepdims=True)
    normed = branch * lax.rsqrt(mean_square + EPSILON) * gain_ref[...][None]
    out_ref[...] = residual_ref[...].astype(jnp.float32) + normed


def sublayer(n, queries, keys, values, residual, post_gain, out_weight):
    kv_heads, _, head_dim = keys.shape
    chips = n // 2
    head_count = queries.shape[1] // head_dim
    own_heads = out_weight.shape[0] // head_dim
    heads = min(head_count // kv_heads, own_heads)
    per_device = own_heads // heads
    width = out_weight.shape[1]
    planes = n // 4
    same_core = [[2 * p + c for p in range(chips)] for c in range(2)]
    same_slot = [[4 * z + slot for z in range(planes)] for slot in range(4)]

    def exchange(x, groups):
        return lax.all_to_all(x, "ctx", 0, 0, axis_index_groups=groups)

    def swap(x, offset):
        return lax.ppermute(x, "ctx", [(i, i ^ offset) for i in range(n)])

    def attended(offset, x, *after):
        return attend(offset, x, keys, values, own_heads, head_count, after)

    own_units = queries.shape[0]
    cover = 4000 * keys.size * keys.dtype.itemsize
    plane = [fetch(queries)] + [swap(queries, offset) for offset in (1, 2, 3)]
    first = exchange(spread(plane, planes, out_weight.shape[0], cover), same_slot)
    first = first.reshape(n * own_units, first.shape[2])
    second = swap(first, 1)
    third = swap(first, 2)
    fourth = swap(third, 1)
    pair = swap(attended(3, first), 1)
    opposite = attended(2, second)
    joined = combine(head_dim, opposite, pair)
    across = swap(joined, 2)
    beside = swap(attended(1, third, joined), 1)
    own = combine(head_dim, attended(0, fourth, joined), beside, across)
    parts = exchange(own.reshape((planes, per_device) + own.shape[1:]), same_slot)
    own_term, other_term = project(parts, out_weight, chips, heads, head_dim)
    term = pl.pallas_call(
        add_kernel,
        out_shape=jax.ShapeDtypeStruct((chips, own_units, width), jnp.bfloat16),
        in_specs=[VMEM_SPEC] * 2,
        out_specs=VMEM_SPEC,
        compiler_params=params(),
    )(own_term, swap(other_term, 1))
    return pl.pallas_call(
        finish_kernel,
        out_shape=jax.ShapeDtypeStruct((own_units, width), jnp.float32),
        in_specs=[VMEM_SPEC] * 3,
        out_specs=VMEM_SPEC,
        compiler_params=params(),
    )(exchange(term, same_core), residual, post_gain)


def solution(mesh):
    in_specs = (
        P(("groups", "ctx"), None),
        P(None, ("groups", "ctx"), None),
        P(None, ("groups", "ctx"), None),
        P(("groups", "ctx"), None),
        P(),
        P("ctx", None),
    )
    out_specs = P(("groups", "ctx"), None)
    return jax.shard_map(
        functools.partial(sublayer, mesh.shape["ctx"]),
        mesh=mesh,
        in_specs=in_specs,
        out_specs=out_specs,
        check_vma=False,
    )
```

```python
import functools
import math

import jax
import jax.numpy as jnp
from jax import lax
from jax.experimental import pallas as pl
from jax.experimental.pallas import tpu as pltpu
from jax.sharding import PartitionSpec as P


SCALE = 168.0 ** (-0.5)
EXPONENT_SCALE = SCALE * math.log2(math.e)
EPSILON = 1e-06
AUX = 8
CHUNK = 2048
VMEM_SPEC = pl.BlockSpec(memory_space=pltpu.VMEM)


def params(limit=8 << 20):
    return pltpu.CompilerParams(vmem_limit_bytes=limit)


def split_pieces(x, count):
    pieces = []
    for _ in range(count):
        piece = x.astype(jnp.bfloat16)
        pieces.append(piece)
        x = x - piece.astype(jnp.float32)
    return pieces


def pack_aux(peak, total):
    rows = split_pieces(peak, 3) + split_pieces(total, 2)
    rows = [row.astype(jnp.float32) for row in rows]
    rows.append(jnp.zeros((AUX - len(rows), peak.shape[1]), jnp.float32))
    return jnp.concatenate(rows, axis=0).astype(jnp.bfloat16)


def unpack_aux(aux):
    aux = aux.astype(jnp.float32)
    peak = (aux[0:1] + aux[1:2]) + aux[2:3]
    total = aux[3:4] + aux[4:5]
    return peak, total


def slot_of(offset):
    return lax.bitwise_xor(lax.rem(lax.axis_index("ctx"), 4), offset)


def fetch_kernel(in_ref, out_ref, sem):
    copy = pltpu.make_async_copy(in_ref, out_ref, sem)
    copy.start()
    copy.wait()


def fetch(x):
    return pl.pallas_call(
        fetch_kernel,
        out_shape=jax.ShapeDtypeStruct(x.shape, x.dtype),
        in_specs=[pl.BlockSpec(memory_space=pltpu.HBM)],
        out_specs=VMEM_SPEC,
        scratch_shapes=[pltpu.SemaphoreType.DMA],
        compiler_params=params(2 << 20),
        cost_estimate=pl.CostEstimate(
            flops=0, bytes_accessed=64 * x.size * x.dtype.itemsize, transcendentals=0
        ),
    )(pltpu.with_memory_space_constraint(x, pltpu.HBM))


def spread_kernel(own_width, own_ref, partner_ref, out_ref):
    chips = out_ref.shape[0]
    slot = slot_of(1)
    parity = lax.rem(slot, 2)
    for p in range(chips):
        start = pl.multiple_of((2 * p + parity) * own_width, own_width)
        own = own_ref[:, pl.ds(start, own_width)].astype(jnp.float32)
        partner = partner_ref[:, pl.ds(start, own_width)].astype(jnp.float32)
        first = jnp.where(parity == 1, own, partner)
        second = jnp.where(parity == 1, partner, own)
        block = jnp.concatenate([first, second], axis=0).astype(jnp.bfloat16)
        for q in range(chips):
            place = p // 2 + (chips // 2 if p % 2 == q % 2 else 0)
            out_ref[q, :, place * own_width : (place + 1) * own_width] = block


def spread(queries, partner_queries, chips, own_width, cover):
    return pl.pallas_call(
        functools.partial(spread_kernel, own_width),
        out_shape=jax.ShapeDtypeStruct(
            (chips, 2 * queries.shape[0], chips * own_width), queries.dtype
        ),
        in_specs=[VMEM_SPEC] * 2,
        out_specs=VMEM_SPEC,
        compiler_params=params(2 << 20),
        cost_estimate=pl.CostEstimate(flops=cover, bytes_accessed=0, transcendentals=0),
    )(queries, partner_queries)


def attend_kernel(
    offset, few, own_heads, heads, group, head_dim, chunk, tasks,
    q_ref, k_ref, v_ref, *refs,
):
    out_ref, score_a, score_b = refs[-3:]
    positions = k_ref.shape[1]
    per_device = own_heads // heads
    slot = slot_of(offset)

    def first_head(t):
        device = 4 * (t // per_device) + slot
        return device * own_heads + (t % per_device) * heads

    def load_query(t):
        first = t * heads + (0 if offset >= 2 else tasks * heads)
        columns = [
            q_ref[:, (first + g) * head_dim : (first + g + 1) * head_dim].astype(jnp.float32)
            for g in range(heads)
        ]
        rows = [
            column[start + core * few : start + (core + 1) * few]
            for core in range(2)
            for column in columns
            for start in range(0, q_ref.shape[0], 2 * few)
        ]
        return jnp.concatenate(rows, axis=0).astype(jnp.bfloat16)

    def score(q, kv, start, score_ref):
        part = lax.dot_general(
            q,
            k_ref[kv, start : start + chunk, :],
            (((1,), (1,)), ((), ())),
            preferred_element_type=jnp.float32,
        )
        score_ref[:, start : start + chunk] = part
        tiles = [part[:, i : i + 128] for i in range(0, chunk, 128)]
        return functools.reduce(jnp.maximum, tiles)

    def weigh(kv, peak, start, score_ref):
        exponent = jnp.exp2((score_ref[:, start : start + chunk] - peak) * EXPONENT_SCALE)
        tiles = [exponent[:, i : i + 128] for i in range(0, chunk, 128)]
        weighted = jnp.dot(
            exponent.astype(jnp.bfloat16),
            v_ref[kv, start : start + chunk, :],
            preferred_element_type=jnp.float32,
        )
        return functools.reduce(jnp.add, tiles), weighted

    def section(t, peak, current_ref, following, next_ref):
        kv = first_head(t) // group
        if following is not None:
            q, next_kv = load_query(following), first_head(following) // group
        highest = total = weighted = None
        for start in range(0, positions, chunk):
            if following is not None:
                part = score(q, next_kv, start, next_ref)
                highest = part if highest is None else jnp.maximum(highest, part)
            exponents, product = weigh(kv, peak, start, current_ref)
            total = exponents if total is None else total + exponents
            weighted = product if weighted is None else weighted + product
        total = jnp.sum(total, axis=1, keepdims=True)
        out_ref[t, 0:head_dim, :] = weighted.T.astype(jnp.bfloat16)
        lane = lax.broadcasted_iota(jnp.int32, (peak.shape[0], 128), 1)
        stats = jnp.where(lane == 0, peak, total).T
        out_ref[t, head_dim : head_dim + AUX, :] = pack_aux(stats[0:1], stats[1:2])
        return None if highest is None else jnp.max(highest, axis=1, keepdims=True)

    q = load_query(0)
    highest = None
    for start in range(0, positions, chunk):
        part = score(q, first_head(0) // group, start, score_a)
        highest = part if highest is None else jnp.maximum(highest, part)
    peak = jnp.max(highest, axis=1, keepdims=True)

    for t in range(tasks):
        score_refs = (score_a, score_b) if t % 2 == 0 else (score_b, score_a)
        peak = section(t, peak, score_refs[0], t + 1 if t + 1 < tasks else None, score_refs[1])


def attend(offset, queries, keys, values, few, own_heads, head_count, after):
    kv_heads, positions, head_dim = keys.shape
    units = queries.shape[0]
    group = head_count // kv_heads
    heads = min(group, own_heads)
    tasks = head_count // (4 * heads)
    rows = units * heads
    return pl.pallas_call(
        functools.partial(
            attend_kernel, offset, few, own_heads, heads, group, head_dim, min(CHUNK, positions), tasks
        ),
        out_shape=jax.ShapeDtypeStruct((tasks, head_dim + AUX, rows), jnp.bfloat16),
        in_specs=[VMEM_SPEC] * (3 + len(after)),
        out_specs=VMEM_SPEC,
        scratch_shapes=[pltpu.VMEM((rows, positions), jnp.float32)] * 2,
        compiler_params=params(20 << 20),
        cost_estimate=pl.CostEstimate(
            flops=4 * tasks * rows * positions * head_dim,
            bytes_accessed=4 * tasks * positions * head_dim,
            transcendentals=tasks * rows * positions,
        ),
    )(queries, keys, values, *after)


def join(head_dim, parts):
    stats = [unpack_aux(part[head_dim : head_dim + AUX, :]) for part in parts]
    peak = functools.reduce(jnp.maximum, [s[0] for s in stats])
    scales = [jnp.exp2((s[0] - peak) * EXPONENT_SCALE) for s in stats]
    total = functools.reduce(jnp.add, [s[1] * x for s, x in zip(stats, scales)])
    weighted = [
        part[0:head_dim, :].astype(jnp.float32) * x for part, x in zip(parts, scales)
    ]
    return peak, total, functools.reduce(jnp.add, weighted)


def combine_kernel(head_dim, *refs):
    out_ref = refs[-1]
    for t in range(out_ref.shape[0]):
        peak, total, weighted = join(head_dim, [ref.at[t] for ref in refs[:-1]])
        out_ref[t, 0:head_dim, :] = weighted.astype(jnp.bfloat16)
        out_ref[t, head_dim : head_dim + AUX, :] = pack_aux(peak, total)


def combine(head_dim, *parts):
    return pl.pallas_call(
        functools.partial(combine_kernel, head_dim),
        out_shape=jax.ShapeDtypeStruct(parts[0].shape, jnp.bfloat16),
        in_specs=[VMEM_SPEC] * len(parts),
        out_specs=VMEM_SPEC,
        compiler_params=params(),
    )(*parts)


def pack_kernel(head_dim, *refs):
    out_ref = refs[-1]
    per_device = out_ref.shape[2]
    half = head_dim // 2
    for t in range(refs[0].shape[0]):
        peak, total, weighted = join(head_dim, [ref.at[t] for ref in refs[:-1]])
        aux = pack_aux(peak, total).astype(jnp.float32)
        units = aux.shape[1] // 2
        for core in range(2):
            lanes = slice(core * units, (core + 1) * units)
            top, bottom = weighted[0:half, lanes], weighted[half:head_dim, lanes]
            cut = out_ref.at[t // per_device, core, t % per_device]
            cut[0:half, :] = jnp.concatenate([top, bottom], axis=1).astype(jnp.bfloat16)
            pair = jnp.concatenate([aux[:, lanes], aux[:, lanes]], axis=1)
            cut[half : half + AUX, :] = pair.astype(jnp.bfloat16)


def pack(head_dim, planes, *parts):
    tasks, _, rows = parts[0].shape
    shape = (planes, 2, tasks // planes, head_dim // 2 + AUX, rows)
    return pl.pallas_call(
        functools.partial(pack_kernel, head_dim),
        out_shape=jax.ShapeDtypeStruct(shape, jnp.bfloat16),
        in_specs=[VMEM_SPEC] * len(parts),
        out_specs=VMEM_SPEC,
        compiler_params=params(),
    )(*parts)


def project_kernel(heads, head_dim, tile, part_ref, weight_ref, partner_ref, out_ref, lhs_ref):
    sources, per_device, _, rows = part_ref.shape
    chips, few, width = out_ref.shape
    half = head_dim // 2
    parity = lax.rem(lax.axis_index("ctx"), 2)
    for side in range(2):
        core = lax.rem(parity + side, 2)
        for j in range(per_device):
            parts = [part_ref.at[2 * z + core, j] for z in range(sources // 2)]
            _, total, weighted = join(half, parts)
            x = weighted / total
            x = jnp.concatenate([x[:, 0 : rows // 2], x[:, rows // 2 : rows]], axis=0).T
            units = x.shape[0] // heads
            for g in range(heads):
                column = (j * heads + g) * head_dim
                lhs_ref[side, :, column : column + head_dim] = x[
                    g * units : (g + 1) * units
                ].astype(jnp.bfloat16)
    own, partner = lhs_ref[0], lhs_ref[1]
    for start in range(0, width, tile):
        columns = slice(start, start + tile)
        out = jnp.dot(own, weight_ref[:, columns], preferred_element_type=jnp.float32)
        out += jnp.dot(partner, partner_ref[:, columns], preferred_element_type=jnp.float32)
        for p in range(chips):
            out_ref[p, :, columns] = out[p * few : (p + 1) * few].astype(jnp.bfloat16)


def project(parts, out_weight, partner_weight, chips, few, heads, head_dim):
    own_width, width = out_weight.shape
    tile = next(t for t in (768, 640, 512, 384, 256, 128, width) if width % t == 0)
    return pl.pallas_call(
        functools.partial(project_kernel, heads, head_dim, tile),
        out_shape=jax.ShapeDtypeStruct((chips, few, width), jnp.bfloat16),
        in_specs=[VMEM_SPEC] * 3,
        out_specs=VMEM_SPEC,
        scratch_shapes=[pltpu.VMEM((2, chips * few, own_width), jnp.bfloat16)],
        compiler_params=params(),
    )(parts, out_weight, partner_weight)


def finish_kernel(terms_ref, residual_ref, gain_ref, out_ref):
    branch = terms_ref[0].astype(jnp.float32)
    for p in range(1, terms_ref.shape[0]):
        branch += terms_ref[p].astype(jnp.float32)
    mean_square = jnp.mean(branch * branch, axis=1, keepdims=True)
    normed = branch * lax.rsqrt(mean_square + EPSILON) * gain_ref[...][None]
    out_ref[...] = residual_ref[...].astype(jnp.float32) + normed


def sublayer(n, queries, keys, values, residual, post_gain, out_weight):
    kv_heads, _, head_dim = keys.shape
    chips = n // 2
    head_count = queries.shape[1] // head_dim
    own_heads = out_weight.shape[0] // head_dim
    heads = min(head_count // kv_heads, own_heads)
    width = out_weight.shape[1]
    planes = n // 4
    same_core = [[2 * p + c for p in range(chips)] for c in range(2)]
    same_side = [
        [4 * z + 2 * y + c for z in range(planes) for c in range(2)] for y in range(2)
    ]

    def exchange(x, groups):
        return lax.all_to_all(x, "ctx", 0, 0, axis_index_groups=groups)

    def swap(x, offset):
        return lax.ppermute(x, "ctx", [(i, i ^ offset) for i in range(n)])

    def attended(offset, x, *after):
        return attend(offset, x, keys, values, own_units, own_heads, head_count, after)

    own_units = queries.shape[0]
    cover = 4000 * keys.size * keys.dtype.itemsize
    partner_queries = swap(queries, 1)
    partner_weight = swap(out_weight, 1)
    ahead = spread(fetch(queries), partner_queries, chips, out_weight.shape[0], cover)
    theirs = exchange(ahead, same_core)
    theirs = theirs.reshape(n * own_units, theirs.shape[2])
    mine = swap(theirs, 1)
    pair = swap(attended(3, theirs), 1)
    joined = combine(head_dim, attended(2, mine), pair)
    across = swap(joined, 2)
    right = attended(1, theirs, joined)
    beside = swap(right, 1)
    own = pack(head_dim, planes, attended(0, mine, right), beside, across)
    parts = exchange(own.reshape((chips,) + own.shape[2:]), same_side)
    term = project(parts, out_weight, partner_weight, chips, own_units, heads, head_dim)
    return pl.pallas_call(
        finish_kernel,
        out_shape=jax.ShapeDtypeStruct((own_units, width), jnp.float32),
        in_specs=[VMEM_SPEC] * 3,
        out_specs=VMEM_SPEC,
        compiler_params=params(),
    )(exchange(term, same_core), residual, post_gain)


def solution(mesh):
    in_specs = (
        P(("groups", "ctx"), None),
        P(None, ("groups", "ctx"), None),
        P(None, ("groups", "ctx"), None),
        P(("groups", "ctx"), None),
        P(),
        P("ctx", None),
    )
    out_specs = P(("groups", "ctx"), None)
    return jax.shard_map(
        functools.partial(sublayer, mesh.shape["ctx"]),
        mesh=mesh,
        in_specs=in_specs,
        out_specs=out_specs,
        check_vma=False,
    )
```

```python
import functools
import math

import jax
import jax.numpy as jnp
from jax import lax
from jax.experimental import pallas as pl
from jax.experimental.pallas import tpu as pltpu
from jax.sharding import PartitionSpec as P


SCALE = 168.0 ** (-0.5)
EXPONENT_SCALE = SCALE * math.log2(math.e)
EPSILON = 1e-06
AUX = 8
CHUNK = 2048
VMEM_SPEC = pl.BlockSpec(memory_space=pltpu.VMEM)


def params(limit=8 << 20):
    return pltpu.CompilerParams(vmem_limit_bytes=limit)


def split_pieces(x, count):
    pieces = []
    for _ in range(count):
        piece = x.astype(jnp.bfloat16)
        pieces.append(piece)
        x = x - piece.astype(jnp.float32)
    return pieces


def pack_aux(peak, total):
    rows = split_pieces(peak, 3) + split_pieces(total, 2)
    rows = [row.astype(jnp.float32) for row in rows]
    rows.append(jnp.zeros((AUX - len(rows), peak.shape[1]), jnp.float32))
    return jnp.concatenate(rows, axis=0).astype(jnp.bfloat16)


def unpack_aux(aux):
    aux = aux.astype(jnp.float32)
    peak = (aux[0:1] + aux[1:2]) + aux[2:3]
    total = aux[3:4] + aux[4:5]
    return peak, total


def slot_of(offset):
    return lax.bitwise_xor(lax.rem(lax.axis_index("ctx"), 4), offset)


def fetch_kernel(in_ref, out_ref, sem):
    copy = pltpu.make_async_copy(in_ref, out_ref, sem)
    copy.start()
    copy.wait()


def fetch(x):
    return pl.pallas_call(
        fetch_kernel,
        out_shape=jax.ShapeDtypeStruct(x.shape, x.dtype),
        in_specs=[pl.BlockSpec(memory_space=pltpu.HBM)],
        out_specs=VMEM_SPEC,
        scratch_shapes=[pltpu.SemaphoreType.DMA],
        compiler_params=params(2 << 20),
        cost_estimate=pl.CostEstimate(
            flops=0, bytes_accessed=64 * x.size * x.dtype.itemsize, transcendentals=0
        ),
    )(pltpu.with_memory_space_constraint(x, pltpu.HBM))


def spread_kernel(own_width, own_ref, partner_ref, out_ref):
    chips = out_ref.shape[0]
    slot = slot_of(1)
    parity = lax.rem(slot, 2)
    for p in range(chips):
        start = pl.multiple_of((2 * p + parity) * own_width, own_width)
        own = own_ref[:, pl.ds(start, own_width)].astype(jnp.float32)
        partner = partner_ref[:, pl.ds(start, own_width)].astype(jnp.float32)
        first = jnp.where(parity == 1, own, partner)
        second = jnp.where(parity == 1, partner, own)
        block = jnp.concatenate([first, second], axis=0).astype(jnp.bfloat16)
        for q in range(chips):
            place = p // 2 + (chips // 2 if p % 2 == q % 2 else 0)
            out_ref[q, :, place * own_width : (place + 1) * own_width] = block


def spread(queries, partner_queries, chips, own_width, cover):
    return pl.pallas_call(
        functools.partial(spread_kernel, own_width),
        out_shape=jax.ShapeDtypeStruct(
            (chips, 2 * queries.shape[0], chips * own_width), queries.dtype
        ),
        in_specs=[VMEM_SPEC] * 2,
        out_specs=VMEM_SPEC,
        compiler_params=params(2 << 20),
        cost_estimate=pl.CostEstimate(flops=cover, bytes_accessed=0, transcendentals=0),
    )(queries, partner_queries)


def attend_kernel(
    offset, few, own_heads, heads, group, head_dim, chunk, tasks, span,
    q_ref, k_ref, v_ref, *refs,
):
    out_ref, score_a, score_b = refs[-3:]
    positions = k_ref.shape[1]
    per_device = own_heads // heads
    slot = slot_of(offset)

    def first_head(t):
        device = 4 * (t // per_device) + slot
        return device * own_heads + (t % per_device) * heads

    def load_query(t):
        first = t * heads + (0 if offset >= 2 else tasks * heads)
        columns = [
            q_ref[:, (first + g) * head_dim : (first + g + 1) * head_dim].astype(jnp.float32)
            for g in range(heads)
        ]
        rows = [
            column[start + core * few : start + (core + 1) * few]
            for core in range(2)
            for column in columns
            for start in range(0, q_ref.shape[0], 2 * few)
        ]
        return jnp.concatenate(rows, axis=0).astype(jnp.bfloat16)

    def score(q, kv, start, score_ref):
        part = lax.dot_general(
            q,
            k_ref[kv, start : start + chunk, :],
            (((1,), (1,)), ((), ())),
            preferred_element_type=jnp.float32,
        )
        score_ref[:, start : start + chunk] = part
        tiles = [part[:, i : i + 128] for i in range(0, chunk, 128)]
        return functools.reduce(jnp.maximum, tiles)

    def weigh(kv, peak, start, score_ref):
        exponent = jnp.exp2((score_ref[:, start : start + chunk] - peak) * EXPONENT_SCALE)
        tiles = [exponent[:, i : i + 128] for i in range(0, chunk, 128)]
        weighted = jnp.dot(
            exponent.astype(jnp.bfloat16),
            v_ref[kv, start : start + chunk, :],
            preferred_element_type=jnp.float32,
        )
        return functools.reduce(jnp.add, tiles), weighted

    def section(t, peak, current_ref, following, next_ref):
        kv = first_head(t) // group
        if following is not None:
            q, next_kv = load_query(following), first_head(following) // group
        highest = total = weighted = None
        for start in range(0, positions, chunk):
            if following is not None:
                part = score(q, next_kv, start, next_ref)
                highest = part if highest is None else jnp.maximum(highest, part)
            exponents, product = weigh(kv, peak, start, current_ref)
            total = exponents if total is None else total + exponents
            weighted = product if weighted is None else weighted + product
        total = jnp.sum(total, axis=1, keepdims=True)
        out_ref[t - span[0], 0:head_dim, :] = weighted.T.astype(jnp.bfloat16)
        lane = lax.broadcasted_iota(jnp.int32, (peak.shape[0], 128), 1)
        stats = jnp.where(lane == 0, peak, total).T
        out_ref[t - span[0], head_dim : head_dim + AUX, :] = pack_aux(stats[0:1], stats[1:2])
        return None if highest is None else jnp.max(highest, axis=1, keepdims=True)

    q = load_query(span[0])
    highest = None
    for start in range(0, positions, chunk):
        part = score(q, first_head(span[0]) // group, start, score_a)
        highest = part if highest is None else jnp.maximum(highest, part)
    peak = jnp.max(highest, axis=1, keepdims=True)

    for t in range(*span):
        score_refs = (score_a, score_b) if (t - span[0]) % 2 == 0 else (score_b, score_a)
        following = t + 1 if t + 1 < span[1] else None
        peak = section(t, peak, score_refs[0], following, score_refs[1])


def attend(offset, queries, keys, values, few, own_heads, head_count, part, after):
    kv_heads, positions, head_dim = keys.shape
    units = queries.shape[0]
    group = head_count // kv_heads
    heads = min(group, own_heads)
    tasks = head_count // (4 * heads)
    rows = units * heads
    span = (0, tasks) if part is None else (part * tasks // 2, (part + 1) * tasks // 2)
    count = span[1] - span[0]
    return pl.pallas_call(
        functools.partial(
            attend_kernel, offset, few, own_heads, heads, group, head_dim, min(CHUNK, positions), tasks, span
        ),
        out_shape=jax.ShapeDtypeStruct((count, head_dim + AUX, rows), jnp.bfloat16),
        in_specs=[VMEM_SPEC] * (3 + len(after)),
        out_specs=VMEM_SPEC,
        scratch_shapes=[pltpu.VMEM((rows, positions), jnp.float32)] * 2,
        compiler_params=params(20 << 20),
        cost_estimate=pl.CostEstimate(
            flops=4 * count * rows * positions * head_dim,
            bytes_accessed=4 * count * positions * head_dim,
            transcendentals=count * rows * positions,
        ),
    )(queries, keys, values, *after)


def join(head_dim, parts):
    stats = [unpack_aux(part[head_dim : head_dim + AUX, :]) for part in parts]
    peak = functools.reduce(jnp.maximum, [s[0] for s in stats])
    scales = [jnp.exp2((s[0] - peak) * EXPONENT_SCALE) for s in stats]
    total = functools.reduce(jnp.add, [s[1] * x for s, x in zip(stats, scales)])
    weighted = [
        part[0:head_dim, :].astype(jnp.float32) * x for part, x in zip(parts, scales)
    ]
    return peak, total, functools.reduce(jnp.add, weighted)


def combine_kernel(head_dim, first, half_ref, whole_ref, out_ref):
    for t in range(out_ref.shape[0]):
        parts = [half_ref.at[t], whole_ref.at[first + t]]
        peak, total, weighted = join(head_dim, parts)
        out_ref[t, 0:head_dim, :] = weighted.astype(jnp.bfloat16)
        out_ref[t, head_dim : head_dim + AUX, :] = pack_aux(peak, total)


def combine(head_dim, first, half, whole):
    return pl.pallas_call(
        functools.partial(combine_kernel, head_dim, first),
        out_shape=jax.ShapeDtypeStruct(half.shape, jnp.bfloat16),
        in_specs=[VMEM_SPEC] * 2,
        out_specs=VMEM_SPEC,
        compiler_params=params(),
    )(half, whole)


def pack_kernel(head_dim, own_ref, beside_ref, first_ref, second_ref, out_ref):
    per_device = out_ref.shape[2]
    half = head_dim // 2
    early = first_ref.shape[0]
    for t in range(own_ref.shape[0]):
        across = first_ref.at[t] if t < early else second_ref.at[t - early]
        peak, total, weighted = join(head_dim, [own_ref.at[t], beside_ref.at[t], across])
        aux = pack_aux(peak, total).astype(jnp.float32)
        units = aux.shape[1] // 2
        for core in range(2):
            lanes = slice(core * units, (core + 1) * units)
            top, bottom = weighted[0:half, lanes], weighted[half:head_dim, lanes]
            cut = out_ref.at[t // per_device, core, t % per_device]
            cut[0:half, :] = jnp.concatenate([top, bottom], axis=1).astype(jnp.bfloat16)
            pair = jnp.concatenate([aux[:, lanes], aux[:, lanes]], axis=1)
            cut[half : half + AUX, :] = pair.astype(jnp.bfloat16)


def pack(head_dim, planes, *parts):
    tasks, _, rows = parts[0].shape
    shape = (planes, 2, tasks // planes, head_dim // 2 + AUX, rows)
    return pl.pallas_call(
        functools.partial(pack_kernel, head_dim),
        out_shape=jax.ShapeDtypeStruct(shape, jnp.bfloat16),
        in_specs=[VMEM_SPEC] * len(parts),
        out_specs=VMEM_SPEC,
        compiler_params=params(),
    )(*parts)


def project_kernel(heads, head_dim, tile, part_ref, weight_ref, partner_ref, out_ref, lhs_ref):
    sources, per_device, _, rows = part_ref.shape
    chips, few, width = out_ref.shape
    half = head_dim // 2
    parity = lax.rem(lax.axis_index("ctx"), 2)
    for side in range(2):
        core = lax.rem(parity + side, 2)
        for j in range(per_device):
            parts = [part_ref.at[2 * z + core, j] for z in range(sources // 2)]
            _, total, weighted = join(half, parts)
            x = weighted / total
            x = jnp.concatenate([x[:, 0 : rows // 2], x[:, rows // 2 : rows]], axis=0).T
            units = x.shape[0] // heads
            for g in range(heads):
                column = (j * heads + g) * head_dim
                lhs_ref[side, :, column : column + head_dim] = x[
                    g * units : (g + 1) * units
                ].astype(jnp.bfloat16)
    own, partner = lhs_ref[0], lhs_ref[1]
    for start in range(0, width, tile):
        columns = slice(start, start + tile)
        out = jnp.dot(own, weight_ref[:, columns], preferred_element_type=jnp.float32)
        out += jnp.dot(partner, partner_ref[:, columns], preferred_element_type=jnp.float32)
        for p in range(chips):
            out_ref[p, :, columns] = out[p * few : (p + 1) * few].astype(jnp.bfloat16)


def project(parts, out_weight, partner_weight, chips, few, heads, head_dim):
    own_width, width = out_weight.shape
    tile = next(t for t in (768, 640, 512, 384, 256, 128, width) if width % t == 0)
    return pl.pallas_call(
        functools.partial(project_kernel, heads, head_dim, tile),
        out_shape=jax.ShapeDtypeStruct((chips, few, width), jnp.bfloat16),
        in_specs=[VMEM_SPEC] * 3,
        out_specs=VMEM_SPEC,
        scratch_shapes=[pltpu.VMEM((2, chips * few, own_width), jnp.bfloat16)],
        compiler_params=params(),
    )(parts, out_weight, partner_weight)


def finish_kernel(terms_ref, residual_ref, gain_ref, out_ref):
    branch = terms_ref[0].astype(jnp.float32)
    for p in range(1, terms_ref.shape[0]):
        branch += terms_ref[p].astype(jnp.float32)
    mean_square = jnp.mean(branch * branch, axis=1, keepdims=True)
    normed = branch * lax.rsqrt(mean_square + EPSILON) * gain_ref[...][None]
    out_ref[...] = residual_ref[...].astype(jnp.float32) + normed


def sublayer(n, queries, keys, values, residual, post_gain, out_weight):
    kv_heads, _, head_dim = keys.shape
    chips = n // 2
    head_count = queries.shape[1] // head_dim
    own_heads = out_weight.shape[0] // head_dim
    heads = min(head_count // kv_heads, own_heads)
    width = out_weight.shape[1]
    planes = n // 4
    same_core = [[2 * p + c for p in range(chips)] for c in range(2)]
    same_side = [
        [4 * z + 2 * y + c for z in range(planes) for c in range(2)] for y in range(2)
    ]

    def exchange(x, groups):
        return lax.all_to_all(x, "ctx", 0, 0, axis_index_groups=groups)

    def swap(x, offset):
        return lax.ppermute(x, "ctx", [(i, i ^ offset) for i in range(n)])

    def attended(offset, x, *after, part=None):
        return attend(
            offset, x, keys, values, own_units, own_heads, head_count, part, after
        )

    own_units = queries.shape[0]
    cover = 4000 * keys.size * keys.dtype.itemsize
    partner_queries = swap(queries, 1)
    partner_weight = swap(out_weight, 1)
    ahead = spread(fetch(queries), partner_queries, chips, out_weight.shape[0], cover)
    theirs = exchange(ahead, same_core)
    theirs = theirs.reshape(n * own_units, theirs.shape[2])
    mine = swap(theirs, 1)
    pair = swap(attended(3, theirs), 1)
    early = attended(2, mine, part=0)
    first = combine(head_dim, 0, early, pair)
    across = [swap(first, 2)]
    late = attended(2, mine, first, part=1)
    second = combine(head_dim, early.shape[0], late, pair)
    across.append(swap(second, 2))
    right = attended(1, theirs, second)
    beside = swap(right, 1)
    own = pack(head_dim, planes, attended(0, mine, right), beside, *across)
    parts = exchange(own.reshape((chips,) + own.shape[2:]), same_side)
    term = project(parts, out_weight, partner_weight, chips, own_units, heads, head_dim)
    return pl.pallas_call(
        finish_kernel,
        out_shape=jax.ShapeDtypeStruct((own_units, width), jnp.float32),
        in_specs=[VMEM_SPEC] * 3,
        out_specs=VMEM_SPEC,
        compiler_params=params(),
    )(exchange(term, same_core), residual, post_gain)


def solution(mesh):
    in_specs = (
        P(("groups", "ctx"), None),
        P(None, ("groups", "ctx"), None),
        P(None, ("groups", "ctx"), None),
        P(("groups", "ctx"), None),
        P(),
        P("ctx", None),
    )
    out_specs = P(("groups", "ctx"), None)
    return jax.shard_map(
        functools.partial(sublayer, mesh.shape["ctx"]),
        mesh=mesh,
        in_specs=in_specs,
        out_specs=out_specs,
        check_vma=False,
    )
```

```python
import functools
import math

import jax
import jax.numpy as jnp
from jax import lax
from jax.experimental import pallas as pl
from jax.experimental.pallas import tpu as pltpu
from jax.sharding import PartitionSpec as P


SCALE = 168.0 ** (-0.5)
EXPONENT_SCALE = SCALE * math.log2(math.e)
EPSILON = 1e-06
AUX = 8
CHUNK = 2048
VMEM_SPEC = pl.BlockSpec(memory_space=pltpu.VMEM)


def params(limit=8 << 20):
    return pltpu.CompilerParams(vmem_limit_bytes=limit)


def split_pieces(x, count):
    pieces = []
    for _ in range(count):
        piece = x.astype(jnp.bfloat16)
        pieces.append(piece)
        x = x - piece.astype(jnp.float32)
    return pieces


def pack_aux(peak, total):
    rows = split_pieces(peak, 3) + split_pieces(total, 2)
    rows = [row.astype(jnp.float32) for row in rows]
    rows.append(jnp.zeros((AUX - len(rows), peak.shape[1]), jnp.float32))
    return jnp.concatenate(rows, axis=0).astype(jnp.bfloat16)


def unpack_aux(aux):
    aux = aux.astype(jnp.float32)
    peak = (aux[0:1] + aux[1:2]) + aux[2:3]
    total = aux[3:4] + aux[4:5]
    return peak, total


def slot_of(offset):
    return lax.bitwise_xor(lax.rem(lax.axis_index("ctx"), 4), offset)


def fetch_kernel(in_ref, out_ref, sem):
    copy = pltpu.make_async_copy(in_ref, out_ref, sem)
    copy.start()
    copy.wait()


def fetch(x):
    return pl.pallas_call(
        fetch_kernel,
        out_shape=jax.ShapeDtypeStruct(x.shape, x.dtype),
        in_specs=[pl.BlockSpec(memory_space=pltpu.HBM)],
        out_specs=VMEM_SPEC,
        scratch_shapes=[pltpu.SemaphoreType.DMA],
        compiler_params=params(2 << 20),
        cost_estimate=pl.CostEstimate(
            flops=0, bytes_accessed=64 * x.size * x.dtype.itemsize, transcendentals=0
        ),
    )(pltpu.with_memory_space_constraint(x, pltpu.HBM))


def spread_kernel(own_width, own_ref, partner_ref, out_ref):
    chips = out_ref.shape[0]
    slot = slot_of(1)
    parity = lax.rem(slot, 2)
    for p in range(chips):
        start = pl.multiple_of((2 * p + parity) * own_width, own_width)
        own = own_ref[:, pl.ds(start, own_width)].astype(jnp.float32)
        partner = partner_ref[:, pl.ds(start, own_width)].astype(jnp.float32)
        first = jnp.where(parity == 1, own, partner)
        second = jnp.where(parity == 1, partner, own)
        block = jnp.concatenate([first, second], axis=0).astype(jnp.bfloat16)
        for q in range(chips):
            place = p // 2 + (chips // 2 if p % 2 == q % 2 else 0)
            out_ref[q, :, place * own_width : (place + 1) * own_width] = block


def spread(queries, partner_queries, chips, own_width, cover):
    return pl.pallas_call(
        functools.partial(spread_kernel, own_width),
        out_shape=jax.ShapeDtypeStruct(
            (chips, 2 * queries.shape[0], chips * own_width), queries.dtype
        ),
        in_specs=[VMEM_SPEC] * 2,
        out_specs=VMEM_SPEC,
        compiler_params=params(2 << 20),
        cost_estimate=pl.CostEstimate(flops=cover, bytes_accessed=0, transcendentals=0),
    )(queries, partner_queries)


def attend_kernel(
    offsets, few, own_heads, heads, group, head_dim, chunk, tasks,
    k_ref, v_ref, *refs,
):
    q_refs, (out_ref, score_a, score_b) = refs[: len(offsets)], refs[-3:]
    positions = k_ref.shape[1]
    per_device = own_heads // heads
    slots = [slot_of(offset) for offset in offsets]

    def first_head(item):
        call, t = divmod(item, tasks)
        device = 4 * (t // per_device) + slots[call]
        return device * own_heads + (t % per_device) * heads

    def load_query(item):
        call, t = divmod(item, tasks)
        q_ref = q_refs[call]
        first = t * heads + (0 if offsets[call] >= 2 else tasks * heads)
        columns = [
            q_ref[:, (first + g) * head_dim : (first + g + 1) * head_dim].astype(jnp.float32)
            for g in range(heads)
        ]
        rows = [
            column[start + core * few : start + (core + 1) * few]
            for core in range(2)
            for column in columns
            for start in range(0, q_ref.shape[0], 2 * few)
        ]
        return jnp.concatenate(rows, axis=0).astype(jnp.bfloat16)

    def score(q, kv, start, score_ref):
        part = lax.dot_general(
            q,
            k_ref[kv, start : start + chunk, :],
            (((1,), (1,)), ((), ())),
            preferred_element_type=jnp.float32,
        )
        score_ref[:, start : start + chunk] = part
        tiles = [part[:, i : i + 128] for i in range(0, chunk, 128)]
        return functools.reduce(jnp.maximum, tiles)

    def weigh(kv, peak, start, score_ref):
        exponent = jnp.exp2((score_ref[:, start : start + chunk] - peak) * EXPONENT_SCALE)
        tiles = [exponent[:, i : i + 128] for i in range(0, chunk, 128)]
        weighted = jnp.dot(
            exponent.astype(jnp.bfloat16),
            v_ref[kv, start : start + chunk, :],
            preferred_element_type=jnp.float32,
        )
        return functools.reduce(jnp.add, tiles), weighted

    def section(t, peak, current_ref, following, next_ref):
        kv = first_head(t) // group
        if following is not None:
            q, next_kv = load_query(following), first_head(following) // group
        highest = total = weighted = None
        for start in range(0, positions, chunk):
            if following is not None:
                part = score(q, next_kv, start, next_ref)
                highest = part if highest is None else jnp.maximum(highest, part)
            exponents, product = weigh(kv, peak, start, current_ref)
            total = exponents if total is None else total + exponents
            weighted = product if weighted is None else weighted + product
        total = jnp.sum(total, axis=1, keepdims=True)
        out_ref[t, 0:head_dim, :] = weighted.T.astype(jnp.bfloat16)
        lane = lax.broadcasted_iota(jnp.int32, (peak.shape[0], 128), 1)
        stats = jnp.where(lane == 0, peak, total).T
        out_ref[t, head_dim : head_dim + AUX, :] = pack_aux(stats[0:1], stats[1:2])
        return None if highest is None else jnp.max(highest, axis=1, keepdims=True)

    q = load_query(0)
    highest = None
    for start in range(0, positions, chunk):
        part = score(q, first_head(0) // group, start, score_a)
        highest = part if highest is None else jnp.maximum(highest, part)
    peak = jnp.max(highest, axis=1, keepdims=True)

    count = len(offsets) * tasks
    for t in range(count):
        score_refs = (score_a, score_b) if t % 2 == 0 else (score_b, score_a)
        peak = section(t, peak, score_refs[0], t + 1 if t + 1 < count else None, score_refs[1])


def attend(offsets, queries, keys, values, few, own_heads, head_count, after):
    kv_heads, positions, head_dim = keys.shape
    units = queries[0].shape[0]
    group = head_count // kv_heads
    heads = min(group, own_heads)
    tasks = head_count // (4 * heads)
    rows = units * heads
    count = len(offsets) * tasks
    return pl.pallas_call(
        functools.partial(
            attend_kernel, offsets, few, own_heads, heads, group, head_dim, min(CHUNK, positions), tasks
        ),
        out_shape=jax.ShapeDtypeStruct((count, head_dim + AUX, rows), jnp.bfloat16),
        in_specs=[VMEM_SPEC] * (2 + len(offsets) + len(after)),
        out_specs=VMEM_SPEC,
        scratch_shapes=[pltpu.VMEM((rows, positions), jnp.float32)] * 2,
        compiler_params=params(20 << 20),
        cost_estimate=pl.CostEstimate(
            flops=4 * count * rows * positions * head_dim,
            bytes_accessed=4 * count * positions * head_dim,
            transcendentals=count * rows * positions,
        ),
    )(keys, values, *queries, *after)


def join(head_dim, parts):
    stats = [unpack_aux(part[head_dim : head_dim + AUX, :]) for part in parts]
    peak = functools.reduce(jnp.maximum, [s[0] for s in stats])
    scales = [jnp.exp2((s[0] - peak) * EXPONENT_SCALE) for s in stats]
    total = functools.reduce(jnp.add, [s[1] * x for s, x in zip(stats, scales)])
    weighted = [
        part[0:head_dim, :].astype(jnp.float32) * x for part, x in zip(parts, scales)
    ]
    return peak, total, functools.reduce(jnp.add, weighted)


def combine_kernel(head_dim, *refs):
    out_ref = refs[-1]
    for t in range(out_ref.shape[0]):
        peak, total, weighted = join(head_dim, [ref.at[t] for ref in refs[:-1]])
        out_ref[t, 0:head_dim, :] = weighted.astype(jnp.bfloat16)
        out_ref[t, head_dim : head_dim + AUX, :] = pack_aux(peak, total)


def combine(head_dim, *parts):
    return pl.pallas_call(
        functools.partial(combine_kernel, head_dim),
        out_shape=jax.ShapeDtypeStruct(parts[0].shape, jnp.bfloat16),
        in_specs=[VMEM_SPEC] * len(parts),
        out_specs=VMEM_SPEC,
        compiler_params=params(),
    )(*parts)


def pack_kernel(head_dim, *refs):
    out_ref = refs[-1]
    per_device = out_ref.shape[2]
    half = head_dim // 2
    both_ref, others = refs[0], refs[1:-1]
    tasks = others[0].shape[0]
    for t in range(tasks):
        parts = [both_ref.at[tasks + t]] + [ref.at[t] for ref in others]
        peak, total, weighted = join(head_dim, parts)
        aux = pack_aux(peak, total).astype(jnp.float32)
        units = aux.shape[1] // 2
        for core in range(2):
            lanes = slice(core * units, (core + 1) * units)
            top, bottom = weighted[0:half, lanes], weighted[half:head_dim, lanes]
            cut = out_ref.at[t // per_device, core, t % per_device]
            cut[0:half, :] = jnp.concatenate([top, bottom], axis=1).astype(jnp.bfloat16)
            pair = jnp.concatenate([aux[:, lanes], aux[:, lanes]], axis=1)
            cut[half : half + AUX, :] = pair.astype(jnp.bfloat16)


def pack(head_dim, planes, *parts):
    tasks, _, rows = parts[1].shape
    shape = (planes, 2, tasks // planes, head_dim // 2 + AUX, rows)
    return pl.pallas_call(
        functools.partial(pack_kernel, head_dim),
        out_shape=jax.ShapeDtypeStruct(shape, jnp.bfloat16),
        in_specs=[VMEM_SPEC] * len(parts),
        out_specs=VMEM_SPEC,
        compiler_params=params(),
    )(*parts)


def project_kernel(heads, head_dim, tile, part_ref, weight_ref, partner_ref, out_ref, lhs_ref):
    sources, per_device, _, rows = part_ref.shape
    chips, few, width = out_ref.shape
    half = head_dim // 2
    parity = lax.rem(lax.axis_index("ctx"), 2)
    for side in range(2):
        core = lax.rem(parity + side, 2)
        for j in range(per_device):
            parts = [part_ref.at[2 * z + core, j] for z in range(sources // 2)]
            _, total, weighted = join(half, parts)
            x = weighted / total
            x = jnp.concatenate([x[:, 0 : rows // 2], x[:, rows // 2 : rows]], axis=0).T
            units = x.shape[0] // heads
            for g in range(heads):
                column = (j * heads + g) * head_dim
                lhs_ref[side, :, column : column + head_dim] = x[
                    g * units : (g + 1) * units
                ].astype(jnp.bfloat16)
    own, partner = lhs_ref[0], lhs_ref[1]
    for start in range(0, width, tile):
        columns = slice(start, start + tile)
        out = jnp.dot(own, weight_ref[:, columns], preferred_element_type=jnp.float32)
        out += jnp.dot(partner, partner_ref[:, columns], preferred_element_type=jnp.float32)
        for p in range(chips):
            out_ref[p, :, columns] = out[p * few : (p + 1) * few].astype(jnp.bfloat16)


def project(parts, out_weight, partner_weight, chips, few, heads, head_dim):
    own_width, width = out_weight.shape
    tile = next(t for t in (768, 640, 512, 384, 256, 128, width) if width % t == 0)
    return pl.pallas_call(
        functools.partial(project_kernel, heads, head_dim, tile),
        out_shape=jax.ShapeDtypeStruct((chips, few, width), jnp.bfloat16),
        in_specs=[VMEM_SPEC] * 3,
        out_specs=VMEM_SPEC,
        scratch_shapes=[pltpu.VMEM((2, chips * few, own_width), jnp.bfloat16)],
        compiler_params=params(),
    )(parts, out_weight, partner_weight)


def finish_kernel(terms_ref, residual_ref, gain_ref, out_ref):
    branch = terms_ref[0].astype(jnp.float32)
    for p in range(1, terms_ref.shape[0]):
        branch += terms_ref[p].astype(jnp.float32)
    mean_square = jnp.mean(branch * branch, axis=1, keepdims=True)
    normed = branch * lax.rsqrt(mean_square + EPSILON) * gain_ref[...][None]
    out_ref[...] = residual_ref[...].astype(jnp.float32) + normed


def sublayer(n, queries, keys, values, residual, post_gain, out_weight):
    kv_heads, _, head_dim = keys.shape
    chips = n // 2
    head_count = queries.shape[1] // head_dim
    own_heads = out_weight.shape[0] // head_dim
    heads = min(head_count // kv_heads, own_heads)
    width = out_weight.shape[1]
    planes = n // 4
    same_core = [[2 * p + c for p in range(chips)] for c in range(2)]
    same_side = [
        [4 * z + 2 * y + c for z in range(planes) for c in range(2)] for y in range(2)
    ]

    def exchange(x, groups):
        return lax.all_to_all(x, "ctx", 0, 0, axis_index_groups=groups)

    def swap(x, offset):
        return lax.ppermute(x, "ctx", [(i, i ^ offset) for i in range(n)])

    def attended(offsets, x, *after):
        return attend(offsets, x, keys, values, own_units, own_heads, head_count, after)

    own_units = queries.shape[0]
    cover = 4000 * keys.size * keys.dtype.itemsize
    partner_queries = swap(queries, 1)
    partner_weight = swap(out_weight, 1)
    ahead = spread(fetch(queries), partner_queries, chips, out_weight.shape[0], cover)
    theirs = exchange(ahead, same_core)
    theirs = theirs.reshape(n * own_units, theirs.shape[2])
    mine = swap(theirs, 1)
    pair = swap(attended((3,), (theirs,)), 1)
    joined = combine(head_dim, attended((2,), (mine,)), pair)
    across = swap(joined, 2)
    both = attended((1, 0), (theirs, mine), joined)
    beside = swap(both[: both.shape[0] // 2], 1)
    own = pack(head_dim, planes, both, beside, across)
    parts = exchange(own.reshape((chips,) + own.shape[2:]), same_side)
    term = project(parts, out_weight, partner_weight, chips, own_units, heads, head_dim)
    return pl.pallas_call(
        finish_kernel,
        out_shape=jax.ShapeDtypeStruct((own_units, width), jnp.float32),
        in_specs=[VMEM_SPEC] * 3,
        out_specs=VMEM_SPEC,
        compiler_params=params(),
    )(exchange(term, same_core), residual, post_gain)


def solution(mesh):
    in_specs = (
        P(("groups", "ctx"), None),
        P(None, ("groups", "ctx"), None),
        P(None, ("groups", "ctx"), None),
        P(("groups", "ctx"), None),
        P(),
        P("ctx", None),
    )
    out_specs = P(("groups", "ctx"), None)
    return jax.shard_map(
        functools.partial(sublayer, mesh.shape["ctx"]),
        mesh=mesh,
        in_specs=in_specs,
        out_specs=out_specs,
        check_vma=False,
    )
```

```python
import functools
import math

import jax
import jax.numpy as jnp
from jax import lax
from jax.experimental import pallas as pl
from jax.experimental.pallas import tpu as pltpu
from jax.sharding import PartitionSpec as P


SCALE = 168.0 ** (-0.5)
EXPONENT_SCALE = SCALE * math.log2(math.e)
EPSILON = 1e-06
AUX = 8
CHUNK = 2048
VMEM_SPEC = pl.BlockSpec(memory_space=pltpu.VMEM)


def params(limit=8 << 20):
    return pltpu.CompilerParams(vmem_limit_bytes=limit)


def split_pieces(x, count):
    pieces = []
    for _ in range(count):
        piece = x.astype(jnp.bfloat16)
        pieces.append(piece)
        x = x - piece.astype(jnp.float32)
    return pieces


def pack_aux(peak, total):
    rows = split_pieces(peak, 3) + split_pieces(total, 2)
    rows = [row.astype(jnp.float32) for row in rows]
    rows.append(jnp.zeros((AUX - len(rows), peak.shape[1]), jnp.float32))
    return jnp.concatenate(rows, axis=0).astype(jnp.bfloat16)


def unpack_aux(aux):
    aux = aux.astype(jnp.float32)
    peak = (aux[0:1] + aux[1:2]) + aux[2:3]
    total = aux[3:4] + aux[4:5]
    return peak, total


def slot_of(offset):
    return lax.bitwise_xor(lax.rem(lax.axis_index("ctx"), 4), offset)


def mark_kernel(out_ref):
    out_ref[...] = jnp.zeros_like(out_ref)


def mark(cover):
    return pl.pallas_call(
        mark_kernel,
        out_shape=jax.ShapeDtypeStruct((8, 128), jnp.float32),
        out_specs=VMEM_SPEC,
        compiler_params=params(2 << 20),
        cost_estimate=pl.CostEstimate(flops=cover, bytes_accessed=0, transcendentals=0),
    )()


def spread_kernel(own_width, own_ref, partner_ref, mark_ref, out_ref):
    chips = out_ref.shape[0]
    slot = slot_of(1)
    parity = lax.rem(slot, 2)
    for p in range(chips):
        start = pl.multiple_of((2 * p + parity) * own_width, own_width)
        own = own_ref[:, pl.ds(start, own_width)].astype(jnp.float32)
        partner = partner_ref[:, pl.ds(start, own_width)].astype(jnp.float32)
        first = jnp.where(parity == 1, own, partner)
        second = jnp.where(parity == 1, partner, own)
        block = jnp.concatenate([first, second], axis=0).astype(jnp.bfloat16)
        for q in range(chips):
            place = p // 2 + (chips // 2 if p % 2 == q % 2 else 0)
            out_ref[q, :, place * own_width : (place + 1) * own_width] = block


def spread(queries, partner_queries, chips, own_width, cover):
    return pl.pallas_call(
        functools.partial(spread_kernel, own_width),
        out_shape=jax.ShapeDtypeStruct(
            (chips, 2 * queries.shape[0], chips * own_width), queries.dtype
        ),
        in_specs=[VMEM_SPEC] * 3,
        out_specs=VMEM_SPEC,
        compiler_params=params(2 << 20),
        cost_estimate=pl.CostEstimate(flops=cover, bytes_accessed=0, transcendentals=0),
    )(queries, partner_queries, mark(cover))


def attend_kernel(
    offsets, few, own_heads, heads, group, head_dim, chunk, tasks,
    k_ref, v_ref, *refs,
):
    q_refs, (out_ref, score_a, score_b) = refs[: len(offsets)], refs[-3:]
    positions = k_ref.shape[1]
    per_device = own_heads // heads
    slots = [slot_of(offset) for offset in offsets]

    def first_head(item):
        call, t = divmod(item, tasks)
        device = 4 * (t // per_device) + slots[call]
        return device * own_heads + (t % per_device) * heads

    def load_query(item):
        call, t = divmod(item, tasks)
        q_ref = q_refs[call]
        first = t * heads + (0 if offsets[call] >= 2 else tasks * heads)
        columns = [
            q_ref[:, (first + g) * head_dim : (first + g + 1) * head_dim].astype(jnp.float32)
            for g in range(heads)
        ]
        rows = [
            column[start + core * few : start + (core + 1) * few]
            for core in range(2)
            for column in columns
            for start in range(0, q_ref.shape[0], 2 * few)
        ]
        return jnp.concatenate(rows, axis=0).astype(jnp.bfloat16)

    def score(q, kv, start, score_ref):
        part = lax.dot_general(
            q,
            k_ref[kv, start : start + chunk, :],
            (((1,), (1,)), ((), ())),
            preferred_element_type=jnp.float32,
        )
        score_ref[:, start : start + chunk] = part
        tiles = [part[:, i : i + 128] for i in range(0, chunk, 128)]
        return functools.reduce(jnp.maximum, tiles)

    def weigh(kv, peak, start, score_ref):
        exponent = jnp.exp2((score_ref[:, start : start + chunk] - peak) * EXPONENT_SCALE)
        tiles = [exponent[:, i : i + 128] for i in range(0, chunk, 128)]
        weighted = jnp.dot(
            exponent.astype(jnp.bfloat16),
            v_ref[kv, start : start + chunk, :],
            preferred_element_type=jnp.float32,
        )
        return functools.reduce(jnp.add, tiles), weighted

    def section(t, peak, current_ref, following, next_ref):
        kv = first_head(t) // group
        if following is not None:
            q, next_kv = load_query(following), first_head(following) // group
        highest = total = weighted = None
        for start in range(0, positions, chunk):
            if following is not None:
                part = score(q, next_kv, start, next_ref)
                highest = part if highest is None else jnp.maximum(highest, part)
            exponents, product = weigh(kv, peak, start, current_ref)
            total = exponents if total is None else total + exponents
            weighted = product if weighted is None else weighted + product
        total = jnp.sum(total, axis=1, keepdims=True)
        out_ref[t, 0:head_dim, :] = weighted.T.astype(jnp.bfloat16)
        lane = lax.broadcasted_iota(jnp.int32, (peak.shape[0], 128), 1)
        stats = jnp.where(lane == 0, peak, total).T
        out_ref[t, head_dim : head_dim + AUX, :] = pack_aux(stats[0:1], stats[1:2])
        return None if highest is None else jnp.max(highest, axis=1, keepdims=True)

    q = load_query(0)
    highest = None
    for start in range(0, positions, chunk):
        part = score(q, first_head(0) // group, start, score_a)
        highest = part if highest is None else jnp.maximum(highest, part)
    peak = jnp.max(highest, axis=1, keepdims=True)

    count = len(offsets) * tasks
    for t in range(count):
        score_refs = (score_a, score_b) if t % 2 == 0 else (score_b, score_a)
        peak = section(t, peak, score_refs[0], t + 1 if t + 1 < count else None, score_refs[1])


def attend(offsets, queries, keys, values, few, own_heads, head_count, after):
    kv_heads, positions, head_dim = keys.shape
    units = queries[0].shape[0]
    group = head_count // kv_heads
    heads = min(group, own_heads)
    tasks = head_count // (4 * heads)
    rows = units * heads
    count = len(offsets) * tasks
    return pl.pallas_call(
        functools.partial(
            attend_kernel, offsets, few, own_heads, heads, group, head_dim, min(CHUNK, positions), tasks
        ),
        out_shape=jax.ShapeDtypeStruct((count, head_dim + AUX, rows), jnp.bfloat16),
        in_specs=[VMEM_SPEC] * (2 + len(offsets) + len(after)),
        out_specs=VMEM_SPEC,
        scratch_shapes=[pltpu.VMEM((rows, positions), jnp.float32)] * 2,
        compiler_params=params(20 << 20),
        cost_estimate=pl.CostEstimate(
            flops=4 * count * rows * positions * head_dim,
            bytes_accessed=4 * count * positions * head_dim,
            transcendentals=count * rows * positions,
        ),
    )(keys, values, *queries, *after)


def join(head_dim, parts):
    stats = [unpack_aux(part[head_dim : head_dim + AUX, :]) for part in parts]
    peak = functools.reduce(jnp.maximum, [s[0] for s in stats])
    scales = [jnp.exp2((s[0] - peak) * EXPONENT_SCALE) for s in stats]
    total = functools.reduce(jnp.add, [s[1] * x for s, x in zip(stats, scales)])
    weighted = [
        part[0:head_dim, :].astype(jnp.float32) * x for part, x in zip(parts, scales)
    ]
    return peak, total, functools.reduce(jnp.add, weighted)


def combine_kernel(head_dim, *refs):
    out_ref = refs[-1]
    for t in range(out_ref.shape[0]):
        peak, total, weighted = join(head_dim, [ref.at[t] for ref in refs[:-1]])
        out_ref[t, 0:head_dim, :] = weighted.astype(jnp.bfloat16)
        out_ref[t, head_dim : head_dim + AUX, :] = pack_aux(peak, total)


def combine(head_dim, *parts):
    return pl.pallas_call(
        functools.partial(combine_kernel, head_dim),
        out_shape=jax.ShapeDtypeStruct(parts[0].shape, jnp.bfloat16),
        in_specs=[VMEM_SPEC] * len(parts),
        out_specs=VMEM_SPEC,
        compiler_params=params(),
    )(*parts)


def pack_kernel(head_dim, *refs):
    out_ref = refs[-1]
    per_device = out_ref.shape[2]
    half = head_dim // 2
    both_ref, others = refs[0], refs[1:-1]
    tasks = others[0].shape[0]
    for t in range(tasks):
        parts = [both_ref.at[tasks + t]] + [ref.at[t] for ref in others]
        peak, total, weighted = join(head_dim, parts)
        aux = pack_aux(peak, total).astype(jnp.float32)
        units = aux.shape[1] // 2
        for core in range(2):
            lanes = slice(core * units, (core + 1) * units)
            top, bottom = weighted[0:half, lanes], weighted[half:head_dim, lanes]
            cut = out_ref.at[t // per_device, core, t % per_device]
            cut[0:half, :] = jnp.concatenate([top, bottom], axis=1).astype(jnp.bfloat16)
            pair = jnp.concatenate([aux[:, lanes], aux[:, lanes]], axis=1)
            cut[half : half + AUX, :] = pair.astype(jnp.bfloat16)


def pack(head_dim, planes, *parts):
    tasks, _, rows = parts[1].shape
    shape = (planes, 2, tasks // planes, head_dim // 2 + AUX, rows)
    return pl.pallas_call(
        functools.partial(pack_kernel, head_dim),
        out_shape=jax.ShapeDtypeStruct(shape, jnp.bfloat16),
        in_specs=[VMEM_SPEC] * len(parts),
        out_specs=VMEM_SPEC,
        compiler_params=params(),
    )(*parts)


def project_kernel(heads, head_dim, tile, part_ref, weight_ref, partner_ref, out_ref, lhs_ref):
    sources, per_device, _, rows = part_ref.shape
    chips, few, width = out_ref.shape
    half = head_dim // 2
    parity = lax.rem(lax.axis_index("ctx"), 2)
    for side in range(2):
        core = lax.rem(parity + side, 2)
        for j in range(per_device):
            parts = [part_ref.at[2 * z + core, j] for z in range(sources // 2)]
            _, total, weighted = join(half, parts)
            x = weighted / total
            x = jnp.concatenate([x[:, 0 : rows // 2], x[:, rows // 2 : rows]], axis=0).T
            units = x.shape[0] // heads
            for g in range(heads):
                column = (j * heads + g) * head_dim
                lhs_ref[side, :, column : column + head_dim] = x[
                    g * units : (g + 1) * units
                ].astype(jnp.bfloat16)
    own, partner = lhs_ref[0], lhs_ref[1]
    for start in range(0, width, tile):
        columns = slice(start, start + tile)
        out = jnp.dot(own, weight_ref[:, columns], preferred_element_type=jnp.float32)
        out += jnp.dot(partner, partner_ref[:, columns], preferred_element_type=jnp.float32)
        for p in range(chips):
            out_ref[p, :, columns] = out[p * few : (p + 1) * few].astype(jnp.bfloat16)


def project(parts, out_weight, partner_weight, chips, few, heads, head_dim):
    own_width, width = out_weight.shape
    tile = next(t for t in (768, 640, 512, 384, 256, 128, width) if width % t == 0)
    return pl.pallas_call(
        functools.partial(project_kernel, heads, head_dim, tile),
        out_shape=jax.ShapeDtypeStruct((chips, few, width), jnp.bfloat16),
        in_specs=[VMEM_SPEC] * 3,
        out_specs=VMEM_SPEC,
        scratch_shapes=[pltpu.VMEM((2, chips * few, own_width), jnp.bfloat16)],
        compiler_params=params(),
    )(parts, out_weight, partner_weight)


def finish_kernel(terms_ref, residual_ref, gain_ref, out_ref):
    branch = terms_ref[0].astype(jnp.float32)
    for p in range(1, terms_ref.shape[0]):
        branch += terms_ref[p].astype(jnp.float32)
    mean_square = jnp.mean(branch * branch, axis=1, keepdims=True)
    normed = branch * lax.rsqrt(mean_square + EPSILON) * gain_ref[...][None]
    out_ref[...] = residual_ref[...].astype(jnp.float32) + normed


def sublayer(n, queries, keys, values, residual, post_gain, out_weight):
    kv_heads, _, head_dim = keys.shape
    chips = n // 2
    head_count = queries.shape[1] // head_dim
    own_heads = out_weight.shape[0] // head_dim
    heads = min(head_count // kv_heads, own_heads)
    width = out_weight.shape[1]
    planes = n // 4
    same_core = [[2 * p + c for p in range(chips)] for c in range(2)]
    same_side = [
        [4 * z + 2 * y + c for z in range(planes) for c in range(2)] for y in range(2)
    ]

    def exchange(x, groups):
        return lax.all_to_all(x, "ctx", 0, 0, axis_index_groups=groups)

    def swap(x, offset):
        return lax.ppermute(x, "ctx", [(i, i ^ offset) for i in range(n)])

    def attended(offsets, x, *after):
        return attend(offsets, x, keys, values, own_units, own_heads, head_count, after)

    own_units = queries.shape[0]
    cover = 4000 * keys.size * keys.dtype.itemsize
    partner_queries = swap(queries, 1)
    partner_weight = swap(out_weight, 1)
    ahead = spread(queries, partner_queries, chips, out_weight.shape[0], cover)
    theirs = exchange(ahead, same_core)
    theirs = theirs.reshape(n * own_units, theirs.shape[2])
    mine = swap(theirs, 1)
    pair = swap(attended((3,), (theirs,)), 1)
    joined = combine(head_dim, attended((2,), (mine,)), pair)
    across = swap(joined, 2)
    both = attended((1, 0), (theirs, mine), joined)
    beside = swap(both[: both.shape[0] // 2], 1)
    own = pack(head_dim, planes, both, beside, across)
    parts = exchange(own.reshape((chips,) + own.shape[2:]), same_side)
    term = project(parts, out_weight, partner_weight, chips, own_units, heads, head_dim)
    return pl.pallas_call(
        finish_kernel,
        out_shape=jax.ShapeDtypeStruct((own_units, width), jnp.float32),
        in_specs=[VMEM_SPEC] * 3,
        out_specs=VMEM_SPEC,
        compiler_params=params(),
    )(exchange(term, same_core), residual, post_gain)


def solution(mesh):
    in_specs = (
        P(("groups", "ctx"), None),
        P(None, ("groups", "ctx"), None),
        P(None, ("groups", "ctx"), None),
        P(("groups", "ctx"), None),
        P(),
        P("ctx", None),
    )
    out_specs = P(("groups", "ctx"), None)
    return jax.shard_map(
        functools.partial(sublayer, mesh.shape["ctx"]),
        mesh=mesh,
        in_specs=in_specs,
        out_specs=out_specs,
        check_vma=False,
    )
```
